256 devices in a mesh: row: 8 (over z_hi, y), col: 32 (over x, z_lo, core).
Axes of the slice: x: 4, y: 4, z: 8 (z_hi: 2, z_lo: 4; z = z_hi * 4 + z_lo), core: 2. Of those that a mesh axis runs over, the one named last changes fastest.
Arguments:
- features: bfloat16 [65536, 256], P('col', 'row'), may hold values from -6 to 6
- block_values: bfloat16 [8, 32, 256, 128, 128], P('row', 'col'), may hold values from -0.046875 to 0.046875
- block_coords: int32 [8, 32, 2, 256], P('row', 'col'), may hold values from 0 to 63, as said below
- live_blocks: int32 [8, 32], P('row', 'col'), may hold values from 32 to 256, as said below
- weight: bfloat16 [256, 256], replicated, may hold values from -0.375 to 0.375
- bias: float32 [256], replicated, may hold values from -3 to 3
- cotangent: bfloat16 [65536, 256], P(('row', 'col')), may hold values from -6 to 6
Outputs:
- out: bfloat16 [65536, 256], P(('row', 'col'))
- grad_x: bfloat16 [65536, 256], P('col', 'row')
- grad_weight: float32 [256, 256], replicated
- grad_bias: float32 [256], replicated
The draws below stay inside these ranges and needn't reach their ends.
Inputs may be any that keep to these rules, and one draw needn't show every extreme that they name: `block_coords`: within one tile the 256 slots name distinct pairs of a row block (0 to 63) and a column block (0 to 15). Only the first live_blocks[i, j] slots of tile (i, j) belong to the adjacency; some tile has all 256 slots live.
All inputs are finite; a program needn't handle non-finite values.
Results may differ from the reference program's by a relative error of at most 0.0075.
Values may be sent and summed in bfloat16 or wider, within the bound.
A program may use at most 128 MiB of HBM per device.

```python
import jax
import jax.numpy as jnp
from jax import lax

F = 256
BS = 128
CB = 16
NB = 256
RB = 64
NODES = 65536
N_ROW = 8
N_COL = 32


def draw_live_blocks(key, part):
    first_key, second_key, third_key = jax.random.split(jax.random.fold_in(key, 11), 3)
    tiles_total = N_ROW * N_COL
    base_counts = jax.random.randint(first_key, (tiles_total,), NB // 8, NB // 2 + 1)
    heavy_tiles = jax.random.randint(second_key, (tiles_total,), 0, 8) == 0
    counts = jnp.where(heavy_tiles, NB, base_counts)
    chosen_tile = jax.random.randint(third_key, (), 0, tiles_total)
    counts = jnp.where(jnp.arange(tiles_total) == chosen_tile, NB, counts)
    return counts.reshape(N_ROW, N_COL).astype(jnp.int32)


def draw_block_coords(key, part):
    tiles_total = N_ROW * N_COL
    positions = RB * CB
    tile_keys = jax.random.split(jax.random.fold_in(key, 23), tiles_total)

    def one_tile(tile_key, tile_number):
        perm_key, slot_key = jax.random.split(tile_key)
        ordering = jax.random.permutation(perm_key, positions)
        target_slot = jax.random.randint(slot_key, (), 0, NB)
        last_place = jnp.argmax(ordering == positions - 1)
        moved = ordering.at[last_place].set(ordering[target_slot]).at[target_slot].set(positions - 1)
        ordering = jnp.where(tile_number == 0, moved, ordering)
        chosen = ordering[:NB]
        return jnp.stack([chosen // CB, chosen % CB])
    coords = jax.vmap(one_tile)(tile_keys, jnp.arange(tiles_total))
    return coords.reshape(N_ROW, N_COL, 2, NB).astype(jnp.int32)


def shard_levels(rng, dims, cuts, least, top_value):
    factor_of = 1.0
    for axis_at, parts in cuts:
        draws = jax.random.uniform(jax.random.fold_in(jax.random.fold_in(rng, 6), axis_at), (parts,), jnp.float32, least / len(cuts), top_value / len(cuts))
        factor_of = factor_of * jnp.repeat(jnp.exp(draws), dims[axis_at] // parts).reshape((-1,) + (1,) * (len(dims) - 1 - axis_at))
    return factor_of


def scatter_about(rng, extent, width, most, pieces=(), kind=jnp.bfloat16):
    entries = width * jax.random.normal(rng, extent, jnp.float32)
    if pieces:
        entries = entries * shard_levels(rng, extent, pieces, -0.22, 0.18)
    return jnp.clip(entries, -most, most).astype(kind)


def setup_inputs(seed: int = 0) -> dict:
    splits = jax.random.split(jax.random.key(seed), 8)
    features = scatter_about(splits[0], (NODES, F), 1.0, 6.0, ((0, 32), (1, 8)))
    block_values = scatter_about(splits[1], (N_ROW, N_COL, NB, BS, BS), (BS * NB * N_COL // RB) ** -0.5, 0.046875, ((0, 8), (1, 32)))
    block_coords = draw_block_coords(jax.random.fold_in(splits[7], 71), 0)
    live_blocks = draw_live_blocks(jax.random.fold_in(splits[7], 71), 0)
    weight = scatter_about(splits[4], (F, F), F ** -0.5, 0.375)
    bias = scatter_about(splits[5], (F,), 0.5, 3.0, (), jnp.float32)
    cotangent = scatter_about(splits[6], (NODES, F), 1.0, 6.0, ((0, 256),))
    return dict(features=features, block_values=block_values, block_coords=block_coords, live_blocks=live_blocks, weight=weight, bias=bias, cotangent=cotangent)


def reference(features, block_values, block_coords, live_blocks, weight, bias, cotangent):
    slot_ids = jnp.arange(NB, dtype=jnp.int32)
    feat_blocks = features.reshape(N_COL, CB, BS, F)

    def forward_row(row_idx):
        def one_tile(totals, col_idx):
            block_vals = block_values[row_idx, col_idx]
            row_ids = block_coords[row_idx, col_idx, 0]
            col_ids = block_coords[row_idx, col_idx, 1]
            alive_mask = slot_ids < live_blocks[row_idx, col_idx]
            picked = jnp.take(feat_blocks[col_idx], col_ids, axis=0)
            products = jnp.einsum('sab,sbf->saf', block_vals.astype(jnp.float32), picked.astype(jnp.float32))
            products = jnp.where(alive_mask[:, None, None], products, 0.0)
            return totals.at[row_ids].add(products), None

        totals, _ = lax.scan(one_tile, jnp.zeros((RB, BS, F), jnp.float32), jnp.arange(N_COL, dtype=jnp.int32))
        return totals

    aggregate = lax.map(forward_row, jnp.arange(N_ROW, dtype=jnp.int32)).reshape(NODES, F).astype(jnp.bfloat16)
    preact = jnp.dot(aggregate, weight, preferred_element_type=jnp.float32) + bias
    sigmoid_v = jax.nn.sigmoid(preact)
    out = (preact * sigmoid_v).astype(jnp.bfloat16)
    derivative = sigmoid_v * (1.0 + preact * (1.0 - sigmoid_v))
    grad_pre = (cotangent.astype(jnp.float32) * derivative).astype(jnp.bfloat16)
    norm_factor = NODES ** -0.5
    grad_weight = jnp.dot(aggregate.T, grad_pre, preferred_element_type=jnp.float32) * norm_factor
    grad_bias = jnp.sum(grad_pre.astype(jnp.float32), axis=0) * norm_factor
    grad_agg = jnp.dot(grad_pre, weight.T, preferred_element_type=jnp.float32).astype(jnp.bfloat16)
    grad_blocks = grad_agg.reshape(N_ROW, RB, BS, F)

    def backward_col(col_idx):
        def one_tile(totals, row_idx):
            block_vals = block_values[row_idx, col_idx]
            row_ids = block_coords[row_idx, col_idx, 0]
            col_ids = block_coords[row_idx, col_idx, 1]
            alive_mask = slot_ids < live_blocks[row_idx, col_idx]
            picked = jnp.take(grad_blocks[row_idx], row_ids, axis=0)
            products = jnp.einsum('sab,saf->sbf', block_vals.astype(jnp.float32), picked.astype(jnp.float32))
            products = jnp.where(alive_mask[:, None, None], products, 0.0)
            return totals.at[col_ids].add(products), None

        totals, _ = lax.scan(one_tile, jnp.zeros((CB, BS, F), jnp.float32), jnp.arange(N_ROW, dtype=jnp.int32))
        return totals

    grad_x = lax.map(backward_col, jnp.arange(N_COL, dtype=jnp.int32)).reshape(NODES, F).astype(jnp.bfloat16)
    return (out, grad_x, grad_weight, grad_bias)
```

```python
import functools

import jax
import jax.numpy as jnp
from jax import lax
from jax.experimental import pallas as pl
from jax.experimental.pallas import tpu as pltpu
from jax.sharding import PartitionSpec as P

MESH = pl.DeviceIdType.MESH
F32 = jnp.float32
BF16 = jnp.bfloat16
VMEM_LIMIT = 64000000
GROUP = 32
UNROLL = 4


def place():
    row, col = lax.axis_index("row"), lax.axis_index("col")
    return row // 4, row % 4, col // 8, (col // 2) % 4, col % 2


def device(zh, y, x, zl, core):
    return (zh * 4 + y, (x * 4 + zl) * 2 + core)


def copy_to(src, dst, sends, recvs, at, dev):
    return pltpu.make_async_remote_copy(
        src_ref=src,
        dst_ref=dst,
        send_sem=sends.at[at],
        recv_sem=recvs.at[at],
        device_id=dev,
        device_id_type=MESH,
    )


def meet(devices):
    barrier = pltpu.get_barrier_semaphore()
    for dev in devices:
        pl.semaphore_signal(barrier, inc=1, device_id=dev, device_id_type=MESH)
    pl.semaphore_wait(barrier, len(devices))


def rem4(v):
    return lax.rem(v, 4)


def gather_rows_kernel(x_ref, full_ref, sends, recvs):
    zh, y, x, zl, core = place()
    right = device(zh, rem4(y + 1), x, zl, core)
    left = device(zh, rem4(y + 3), x, zl, core)
    across = device(1 - zh, y, x, zl, core)
    meet((left, right, across))
    mine = zh * 4 + y
    other = (1 - zh) * 4 + y
    halves = (pl.ds(0, 16), pl.ds(16, 16))
    started = []

    def start(c):
        c.start()
        started.append(c)
        return c

    zc = [
        start(copy_to(x_ref.at[h], full_ref.at[mine, h], sends, recvs, 12 + i, across))
        for i, h in enumerate(halves)
    ]
    full_ref[mine] = x_ref[...]
    firsts = []
    for k in range(2):
        me = mine if k == 0 else other
        base = (zh if k == 0 else 1 - zh) * 4
        src = x_ref if k == 0 else full_ref.at[other]

        def ring(h, at, dev):
            return start(
                copy_to(src.at[halves[h]], full_ref.at[me, halves[h]], sends, recvs, k * 6 + at, dev)
            )

        if k == 1:
            zc[0].wait_recv()
        r0 = ring(0, 0, right)
        if k == 1:
            zc[1].wait_recv()
        l1 = ring(1, 1, left)
        r1 = ring(1, 2, right)
        l0 = ring(0, 3, left)
        firsts.append((r0, l1, r1, l0, base))
        if k == 0:
            continue
    forwards = []
    for k in range(2):
        r0, l1, r1, l0, base = firsts[k]
        from_left = base + rem4(y + 3)
        from_right = base + rem4(y + 1)
        r0.wait_recv()
        fr = start(
            copy_to(
                full_ref.at[from_left, halves[0]],
                full_ref.at[from_left, halves[0]],
                sends,
                recvs,
                k * 6 + 4,
                right,
            )
        )
        l1.wait_recv()
        fl = start(
            copy_to(
                full_ref.at[from_right, halves[1]],
                full_ref.at[from_right, halves[1]],
                sends,
                recvs,
                k * 6 + 5,
                left,
            )
        )
        forwards += [r1, l0, fr, fl]
    for c in forwards:
        c.wait_recv()
    for c in started:
        c.wait_send()


def gather_rows(x_t):
    width, verts = x_t.shape
    return pl.pallas_call(
        gather_rows_kernel,
        out_shape=jax.ShapeDtypeStruct((8, width, verts), BF16),
        in_specs=[pl.BlockSpec(memory_space=pltpu.VMEM)],
        out_specs=pl.BlockSpec(memory_space=pltpu.VMEM),
        scratch_shapes=[pltpu.SemaphoreType.DMA((14,)), pltpu.SemaphoreType.DMA((14,))],
        compiler_params=pltpu.CompilerParams(
            collective_id=0, has_side_effects=True, vmem_limit_bytes=VMEM_LIMIT
        ),
        name="gather_features",
    )(x_t)


def forward_kernel(rows, cols, live, a_ref, xt_ref, out_ref, xs, acc):
    g = pl.program_id(0)
    n_rb = acc.shape[0] - 1
    n_cb = xs.shape[0]

    @pl.when(g == 0)
    def _():
        for c in range(n_cb):
            xs[c] = xt_ref[:, c * 128 : (c + 1) * 128].T

        def clear(i, _):
            acc[i] = jnp.zeros(acc.shape[1:], F32)
            return 0

        lax.fori_loop(0, n_rb, clear, 0)

    count = jnp.clip(live[0] - g * GROUP, 0, GROUP)

    def some(q, _):
        products = []
        for u in range(UNROLL):
            s = q * UNROLL + u
            products.append(
                jnp.dot(a_ref[s], xs[cols[g * GROUP + s]], preferred_element_type=F32)
            )
        for u in range(UNROLL):
            s = g * GROUP + q * UNROLL + u
            r = jnp.where(s < live[0], rows[s], n_rb)
            acc[r] += products[u]
        return 0

    lax.fori_loop(0, (count + UNROLL - 1) // UNROLL, some, 0)

    @pl.when(g == pl.num_programs(0) - 1)
    def _():
        def put(chip, _):
            for k in range(4):
                out_ref[k // 2, chip, (k % 2) * 128 : (k % 2 + 1) * 128, :] = acc[chip * 4 + k].astype(BF16)
            return 0

        lax.fori_loop(0, 16, put, 0)


def forward_products(rows, cols, live, blocks, x_t):
    n_slots = blocks.shape[0]
    return pl.pallas_call(
        forward_kernel,
        out_shape=jax.ShapeDtypeStruct((2, 16, 256, 256), BF16),
        grid_spec=pltpu.PrefetchScalarGridSpec(
            num_scalar_prefetch=3,
            grid=(n_slots // GROUP,),
            in_specs=[
                pl.BlockSpec((GROUP, 128, 128), lambda g, *_: (g, 0, 0)),
                pl.BlockSpec((256, 2048), lambda g, *_: (0, 0)),
            ],
            out_specs=pl.BlockSpec((2, 16, 256, 256), lambda g, *_: (0, 0, 0, 0)),
            scratch_shapes=[pltpu.VMEM((16, 128, 256), BF16), pltpu.VMEM((65, 128, 256), F32)],
        ),
        compiler_params=pltpu.CompilerParams(vmem_limit_bytes=VMEM_LIMIT),
        name="forward_products",
    )(rows, cols, live, blocks, x_t)


def middle_kernel(
    part, cot_ref, w_ref, bias_ref, out_ref, full_ref, term_ref,
    r_a, s_a, r_b1l, r_b1r, r_b2l, r_b2r, s_b, r_c, sends, recvs,
):
    zh, y, x, zl, core = place()
    right = device(zh, y, rem4(x + 1), zl, core)
    left = device(zh, y, rem4(x + 3), zl, core)
    twin = device(zh, y, x, zl, 1 - core)
    along = [None] + [device(zh, y, x, rem4(zl + k), core) for k in range(1, 4)]
    meet((left, right, twin, along[1], along[2], along[3]))
    started = []
    used = [0]

    def start(src, dst, dev):
        c = copy_to(src, dst, sends, recvs, used[0], dev)
        used[0] += 1
        c.start()
        started.append(c)
        return c

    top, low = pl.ds(0, 128), pl.ds(128, 128)
    xk = [rem4(x + k) for k in range(4)]
    zk = [rem4(zl + k) for k in range(4)]
    order = (1, 2, 3, 0)
    a = {}
    for k in (2, 1, 3, 0):
        sl = pl.ds(xk[k] * 4, 4)
        a[k] = start(part.at[1 - core, sl], r_a.at[sl], twin)

    def add_cores(k):
        a[k].wait_recv()

        def one(z, _):
            i = xk[k] * 4 + z
            s_a[i] = (part[core, i].astype(F32) + r_a[i].astype(F32)).astype(BF16)
            return 0

        lax.fori_loop(0, 4, one, 0)

    add_cores(2)
    b1 = {}
    for k in order:
        i = xk[2] * 4 + zk[k]
        b1[k] = (
            start(s_a.at[i, top], r_b1l.at[k], right),
            start(s_a.at[i, low], r_b1r.at[k], left),
        )
    b2 = {}
    add_cores(1)
    for k in order:
        b2[k] = [start(s_a.at[xk[1] * 4 + zk[k], low], r_b2l.at[k, low], right)]
    add_cores(3)
    for k in order:
        b2[k].append(start(s_a.at[xk[3] * 4 + zk[k], top], r_b2r.at[k, top], left))
    for k in order:
        b1[k][0].wait_recv()
        i = xk[1] * 4 + zk[k]
        s_a[i, top] = (s_a[i, top].astype(F32) + r_b1l[k].astype(F32)).astype(BF16)
        b2[k].append(start(s_a.at[i, top], r_b2l.at[k, top], right))
        b1[k][1].wait_recv()
        j = xk[3] * 4 + zk[k]
        s_a[j, low] = (s_a[j, low].astype(F32) + r_b1r[k].astype(F32)).astype(BF16)
        b2[k].append(start(s_a.at[j, low], r_b2r.at[k, low], left))
    add_cores(0)
    c_z = {}
    total = None
    for k in order:
        for c in b2[k]:
            c.wait_recv()
        i = x * 4 + zk[k]
        value = s_a[i].astype(F32) + (r_b2l[k].astype(F32) + r_b2r[k].astype(F32))
        if k == 0:
            total = value
        else:
            s_b[k] = value.astype(BF16)
            c_z[k] = start(s_b.at[k], r_c.at[k], along[k])
    for k in (1, 2, 3):
        c_z[k].wait_recv()
        total = total + r_c[k].astype(F32)
    aggregate = total.astype(BF16)
    preact = jnp.dot(aggregate, w_ref[...], preferred_element_type=F32) + bias_ref[...]
    sig = jax.nn.sigmoid(preact)
    derivative = sig * (1.0 + preact * (1.0 - sig))
    grad_pre = (cot_ref[...].astype(F32) * derivative).astype(BF16)
    grad_agg = lax.dot_general(
        w_ref[...], grad_pre, (((1,), (1,)), ((), ())), preferred_element_type=F32
    ).astype(BF16)
    mine = (x * 4 + zl) * 2 + core
    full_ref[mine, 0] = grad_agg[:, 0:128]
    full_ref[mine, 1] = grad_agg[:, 128:256]

    def at(xx, zz):
        return (xx * 4 + zz) * 2 + core

    def ring(d):
        here = full_ref
        return (
            start(here.at[d, 0], here.at[d, 0], right),
            start(here.at[d, 1], here.at[d, 1], left),
            start(here.at[d, 1], here.at[d, 1], right),
            start(here.at[d, 0], here.at[d, 0], left),
        )

    def same(d, dev):
        return start(full_ref.at[d], full_ref.at[d], dev)

    def same_half(d, h, dev):
        return start(full_ref.at[d, h], full_ref.at[d, h], dev)

    z_in = {k: same(mine, along[k]) for k in (1, 2, 3)}
    rings = {0: ring(mine)}
    twins = [same(mine, twin)]
    zb = [rem4(zl + 4 - k) for k in range(4)]

    out_ref[...] = (preact * sig).astype(BF16)
    term_ref[:, 0:256] = lax.dot_general(
        aggregate, grad_pre, (((0,), (0,)), ((), ())), preferred_element_type=F32
    )
    term_ref[:, 256:384] = lax.dot_general(
        grad_pre, jnp.ones((256, 128), BF16), (((0,), (0,)), ((), ())), preferred_element_type=F32
    )

    forwards = {}

    def relay(k):
        dl, dr = at(xk[3], zb[k]), at(xk[1], zb[k])
        rings[k][0].wait_recv()
        fr = same_half(dl, 0, right)
        rings[k][1].wait_recv()
        fl = same_half(dr, 1, left)
        forwards[k] = (fr, fl)

    def hand_over(k):
        dl, dr = at(xk[3], zb[k]), at(xk[1], zb[k])
        rings[k][2].wait_recv()
        twins.append(same(dl, twin))
        rings[k][3].wait_recv()
        twins.append(same(dr, twin))

    for k in range(4):
        if k < 3:
            d = at(x, zb[k + 1])
            z_in[k + 1].wait_recv()
            rings[k + 1] = ring(d)
            twins.append(same(d, twin))
        relay(k)
        hand_over(k)
    for k in range(4):
        d = at(xk[2], zb[k])
        forwards[k][0].wait_recv()
        twins.append(same_half(d, 0, twin))
        forwards[k][1].wait_recv()
        twins.append(same_half(d, 1, twin))
    for c in twins:
        c.wait_recv()
    for c in started:
        c.wait_send()


def middle(part, cot, weight, bias):
    vmem = pl.BlockSpec(memory_space=pltpu.VMEM)
    chunk = (256, 256)
    return pl.pallas_call(
        middle_kernel,
        out_shape=(
            jax.ShapeDtypeStruct(chunk, BF16),
            jax.ShapeDtypeStruct((32, 2, 256, 128), BF16),
            jax.ShapeDtypeStruct((256, 384), F32),
        ),
        in_specs=[vmem] * 4,
        out_specs=(vmem,) * 3,
        scratch_shapes=[
            pltpu.VMEM((16,) + chunk, BF16),
            pltpu.VMEM((16,) + chunk, BF16),
            pltpu.VMEM((4, 128, 256), BF16),
            pltpu.VMEM((4, 128, 256), BF16),
            pltpu.VMEM((4,) + chunk, BF16),
            pltpu.VMEM((4,) + chunk, BF16),
            pltpu.VMEM((4,) + chunk, BF16),
            pltpu.VMEM((4,) + chunk, BF16),
            pltpu.SemaphoreType.DMA((96,)),
            pltpu.SemaphoreType.DMA((96,)),
        ],
        compiler_params=pltpu.CompilerParams(
            collective_id=1, has_side_effects=True, vmem_limit_bytes=VMEM_LIMIT
        ),
        name="layer",
    )(part, cot, weight, bias)


def backward_kernel(rows, cols, live, a_ref, g_ref, out_ref, acc):
    g = pl.program_id(0)
    n_cb = acc.shape[0] - 1

    @pl.when(g == 0)
    def _():
        def clear(i, _):
            acc[i] = jnp.zeros(acc.shape[1:], F32)
            return 0

        lax.fori_loop(0, n_cb, clear, 0)

    count = jnp.clip(live[0] - g * GROUP, 0, GROUP)

    def some(q, _):
        products = []
        for u in range(UNROLL):
            s = q * UNROLL + u
            products.append(
                jnp.dot(g_ref[rows[g * GROUP + s]], a_ref[s], preferred_element_type=F32)
            )
        for u in range(UNROLL):
            s = g * GROUP + q * UNROLL + u
            c = jnp.where(s < live[0], cols[s], n_cb)
            acc[c] += products[u]
        return 0

    lax.fori_loop(0, (count + UNROLL - 1) // UNROLL, some, 0)

    @pl.when(g == pl.num_programs(0) - 1)
    def _():
        for c in range(n_cb):
            out_ref[:, c * 128 : (c + 1) * 128] = acc[c].astype(BF16)


def backward_products(rows, cols, live, blocks, grads):
    n_slots = blocks.shape[0]
    return pl.pallas_call(
        backward_kernel,
        out_shape=jax.ShapeDtypeStruct((256, 2048), BF16),
        grid_spec=pltpu.PrefetchScalarGridSpec(
            num_scalar_prefetch=3,
            grid=(n_slots // GROUP,),
            in_specs=[
                pl.BlockSpec((GROUP, 128, 128), lambda g, *_: (g, 0, 0)),
                pl.BlockSpec((64, 256, 128), lambda g, *_: (0, 0, 0)),
            ],
            out_specs=pl.BlockSpec((256, 2048), lambda g, *_: (0, 0)),
            scratch_shapes=[pltpu.VMEM((17, 256, 128), F32)],
        ),
        compiler_params=pltpu.CompilerParams(vmem_limit_bytes=VMEM_LIMIT),
        name="backward_products",
    )(rows, cols, live, blocks, grads)


def finish_kernel(
    norm, part, term_ref, gx_ref, gw_ref, gb_ref,
    r_b1l, r_b1r, s_b1r, s_b1l, r_b2l, r_b2r, s_b, r_c,
    t_c, u_c, t_x, u_x, t_y, u_y, t_z, all_t, sends, recvs,
):
    zh, y, x, zl, core = place()
    right = device(zh, rem4(y + 1), x, zl, core)
    left = device(zh, rem4(y + 3), x, zl, core)
    across = device(1 - zh, y, x, zl, core)
    twin = device(zh, y, x, zl, 1 - core)
    y_dev = [None] + [device(zh, rem4(y + k), x, zl, core) for k in range(1, 4)]
    x_dev = [None] + [device(zh, y, rem4(x + k), zl, core) for k in range(1, 4)]
    zz = zh * 4 + zl
    z_dev = [None]
    for k in range(1, 8):
        other = lax.rem(zz + k, 8)
        z_dev.append(device(other // 4, y, x, lax.rem(other, 4), core))
    meet([twin] + y_dev[1:] + x_dev[1:] + z_dev[1:])
    started = []
    used = [0]

    def start(src, dst, dev):
        c = copy_to(src, dst, sends, recvs, used[0], dev)
        used[0] += 1
        c.start()
        started.append(c)
        return c

    yk = [rem4(y + k) for k in range(4)]
    xk = [rem4(x + k) for k in range(4)]
    top, low = pl.ds(0, 16), pl.ds(16, 16)

    def parameters():
        half = pl.ds(pl.multiple_of(core * 128, 128), 128)
        c = start(term_ref.at[pl.ds(pl.multiple_of((1 - core) * 128, 128), 128)], t_c, twin)
        yield
        c.wait_recv()
        u_c[...] = term_ref[half] + t_c[...]
        cs = [
            start(u_c.at[pl.ds(pl.multiple_of(xk[k] * 32, 32), 32)], t_x.at[k], x_dev[k])
            for k in (2, 1, 3)
        ]
        yield
        for c in cs:
            c.wait_recv()
        u_x[...] = u_c[pl.ds(pl.multiple_of(x * 32, 32), 32)] + (t_x[1] + t_x[2] + t_x[3])
        cs = [
            start(u_x.at[pl.ds(pl.multiple_of(yk[k] * 8, 8), 8)], t_y.at[k], y_dev[k])
            for k in (2, 1, 3)
        ]
        yield
        for c in cs:
            c.wait_recv()
        u_y[...] = u_x[pl.ds(pl.multiple_of(y * 8, 8), 8)] + (t_y[1] + t_y[2] + t_y[3])
        cs = [start(u_y, t_z.at[zz], z_dev[k]) for k in (4, 3, 5, 2, 6, 1, 7)]
        t_z[zz] = u_y[...]
        yield
        for c in cs:
            c.wait_recv()
        value = t_z[0]
        for k in range(1, 8):
            value = value + t_z[k]
        spot = pl.ds(pl.multiple_of(core * 128 + x * 32 + y * 8, 8), 8)
        all_t[spot] = value * norm
        cs = [start(all_t.at[spot], all_t.at[spot], y_dev[k]) for k in (2, 1, 3)]
        yield
        for c in cs:
            c.wait_recv()
        spot = pl.ds(pl.multiple_of(core * 128 + x * 32, 32), 32)
        cs = [start(all_t.at[spot], all_t.at[spot], x_dev[k]) for k in (2, 1, 3)]
        yield
        for c in cs:
            c.wait_recv()
        c = start(all_t.at[half], all_t.at[half], twin)
        yield
        c.wait_recv()
        gw_ref[...] = all_t[:, 0:256]
        gb_ref[...] = all_t[:, 256:384]
        yield

    params = parameters()
    next(params)
    zs = (1 - zh, zh)
    b1, b2 = [], []
    for j in range(2):
        i = zs[j] * 4 + yk[2]
        b1.append(
            (start(part.at[i, top], r_b1l.at[j], right), start(part.at[i, low], r_b1r.at[j], left))
        )
        b2.append(
            [
                start(part.at[zs[j] * 4 + yk[1], low], r_b2l.at[j, low], right),
                start(part.at[zs[j] * 4 + yk[3], top], r_b2r.at[j, top], left),
            ]
        )
    next(params)
    for j in range(2):
        b1[j][0].wait_recv()
        s_b1r[j] = (part[zs[j] * 4 + yk[1], top].astype(F32) + r_b1l[j].astype(F32)).astype(BF16)
        b2[j].append(start(s_b1r.at[j], r_b2l.at[j, top], right))
        b1[j][1].wait_recv()
        s_b1l[j] = (part[zs[j] * 4 + yk[3], low].astype(F32) + r_b1r[j].astype(F32)).astype(BF16)
        b2[j].append(start(s_b1l.at[j], r_b2r.at[j, low], left))
    next(params)

    def summed(j):
        for c in b2[j]:
            c.wait_recv()
        return part[zs[j] * 4 + y].astype(F32) + (r_b2l[j].astype(F32) + r_b2r[j].astype(F32))

    s_b[...] = summed(0).astype(BF16)
    cz = start(s_b, r_c, across)
    next(params)
    own = summed(1)
    cz.wait_recv()
    gx_ref[...] = (own + r_c[...].astype(F32)).astype(BF16)
    for _ in params:
        pass
    for c in started:
        c.wait_send()


def finish(part, term, norm):
    vmem = pl.BlockSpec(memory_space=pltpu.VMEM)
    half, whole = (2, 16, 2048), (2, 32, 2048)
    return pl.pallas_call(
        functools.partial(finish_kernel, norm),
        out_shape=(
            jax.ShapeDtypeStruct((32, 2048), BF16),
            jax.ShapeDtypeStruct((256, 256), F32),
            jax.ShapeDtypeStruct((256, 128), F32),
        ),
        in_specs=[vmem] * 2,
        out_specs=(vmem,) * 3,
        scratch_shapes=[
            pltpu.VMEM(half, BF16),
            pltpu.VMEM(half, BF16),
            pltpu.VMEM(half, BF16),
            pltpu.VMEM(half, BF16),
            pltpu.VMEM(whole, BF16),
            pltpu.VMEM(whole, BF16),
            pltpu.VMEM(whole[1:], BF16),
            pltpu.VMEM(whole[1:], BF16),
            pltpu.VMEM((128, 384), F32),
            pltpu.VMEM((128, 384), F32),
            pltpu.VMEM((4, 32, 384), F32),
            pltpu.VMEM((32, 384), F32),
            pltpu.VMEM((4, 8, 384), F32),
            pltpu.VMEM((8, 384), F32),
            pltpu.VMEM((8, 8, 384), F32),
            pltpu.VMEM((256, 384), F32),
            pltpu.SemaphoreType.DMA((40,)),
            pltpu.SemaphoreType.DMA((40,)),
        ],
        compiler_params=pltpu.CompilerParams(
            collective_id=2, has_side_effects=True, vmem_limit_bytes=VMEM_LIMIT
        ),
        name="finish",
    )(part, term)


def on_device(features, block_values, block_coords, live_blocks, weight, bias, cotangent):
    blocks = block_values[0, 0]
    rows, cols = block_coords[0, 0, 0], block_coords[0, 0, 1]
    live = live_blocks[0]
    nodes = features.shape[0] * lax.axis_size("col")
    x_t = gather_rows(features.T).reshape(256, 2048)
    part = forward_products(rows, cols, live, blocks, x_t)
    out, grads, term = middle(part, cotangent, weight, bias[None])
    part_x = backward_products(rows, cols, live, blocks, grads.reshape(64, 256, 128))
    gx_t, grad_weight, grad_bias = finish(part_x.reshape(8, 32, 2048), term, nodes**-0.5)
    return out, gx_t.T, grad_weight, grad_bias[:, 0]


def solution(mesh):
    in_specs = (
        P("col", "row"),
        P("row", "col", None, None, None),
        P("row", "col", None, None),
        P("row", "col"),
        P(),
        P(),
        P(("row", "col"), None),
    )
    out_specs = (P(("row", "col"), None), P("col", "row"), P(), P())
    return jax.shard_map(
        on_device, mesh=mesh, in_specs=in_specs, out_specs=out_specs, check_vma=False
    )
```

```python
import functools

import jax
import jax.numpy as jnp
from jax import lax
from jax.experimental import pallas as pl
from jax.experimental.pallas import tpu as pltpu
from jax.sharding import PartitionSpec as P

MESH = pl.DeviceIdType.MESH
F32 = jnp.float32
BF16 = jnp.bfloat16
UNROLL = 4
VMEM = pl.BlockSpec(memory_space=pltpu.VMEM)
SMEM = pl.BlockSpec(memory_space=pltpu.SMEM)
MIB = 2**20
GATHER_VMEM = 4 * MIB
FORWARD_VMEM = 24 * MIB
MIDDLE_VMEM = 24 * MIB
BACKWARD_VMEM = 20 * MIB
FINISH_VMEM = 6 * MIB


def place():
    row, col = lax.axis_index("row"), lax.axis_index("col")
    return row // 4, row % 4, col // 8, (col // 2) % 4, col % 2


def device(zh, y, x, zl, core):
    return (zh * 4 + y, (x * 4 + zl) * 2 + core)


def copy_to(src, dst, sends, recvs, at, dev):
    return pltpu.make_async_remote_copy(
        src_ref=src,
        dst_ref=dst,
        send_sem=sends.at[at],
        recv_sem=recvs.at[at],
        device_id=dev,
        device_id_type=MESH,
    )


def meet(devices):
    barrier = pltpu.get_barrier_semaphore()
    for dev in devices:
        pl.semaphore_signal(barrier, inc=1, device_id=dev, device_id_type=MESH)
    pl.semaphore_wait(barrier, len(devices))


def rem4(v):
    return lax.rem(v, 4)


def gather_rows_kernel(x_ref, full_ref, sends, recvs):
    zh, y, x, zl, core = place()
    right = device(zh, rem4(y + 1), x, zl, core)
    left = device(zh, rem4(y + 3), x, zl, core)
    across = device(1 - zh, y, x, zl, core)
    meet((left, right, across))
    mine = zh * 4 + y
    other = (1 - zh) * 4 + y
    halves = (pl.ds(0, 16), pl.ds(16, 16))
    started = []

    def start(c):
        c.start()
        started.append(c)
        return c

    zc = [
        start(copy_to(x_ref.at[h], full_ref.at[mine, h], sends, recvs, 12 + i, across))
        for i, h in enumerate(halves)
    ]
    full_ref[mine] = x_ref[...]
    firsts = []
    for k in range(2):
        me = mine if k == 0 else other
        base = (zh if k == 0 else 1 - zh) * 4
        src = x_ref if k == 0 else full_ref.at[other]

        def ring(h, at, dev):
            return start(
                copy_to(src.at[halves[h]], full_ref.at[me, halves[h]], sends, recvs, k * 6 + at, dev)
            )

        if k == 1:
            zc[0].wait_recv()
        r0 = ring(0, 0, right)
        if k == 1:
            zc[1].wait_recv()
        l1 = ring(1, 1, left)
        r1 = ring(1, 2, right)
        l0 = ring(0, 3, left)
        firsts.append((r0, l1, r1, l0, base))
        if k == 0:
            continue
    forwards = []
    for k in range(2):
        r0, l1, r1, l0, base = firsts[k]
        from_left = base + rem4(y + 3)
        from_right = base + rem4(y + 1)
        r0.wait_recv()
        fr = start(
            copy_to(
                full_ref.at[from_left, halves[0]],
                full_ref.at[from_left, halves[0]],
                sends,
                recvs,
                k * 6 + 4,
                right,
            )
        )
        l1.wait_recv()
        fl = start(
            copy_to(
                full_ref.at[from_right, halves[1]],
                full_ref.at[from_right, halves[1]],
                sends,
                recvs,
                k * 6 + 5,
                left,
            )
        )
        forwards += [r1, l0, fr, fl]
    for c in forwards:
        c.wait_recv()
    for c in started:
        c.wait_send()


def gather_rows(x_t):
    width, verts = x_t.shape
    return pl.pallas_call(
        gather_rows_kernel,
        out_shape=jax.ShapeDtypeStruct((8, width, verts), BF16),
        in_specs=[pl.BlockSpec(memory_space=pltpu.VMEM)],
        out_specs=pl.BlockSpec(memory_space=pltpu.VMEM),
        scratch_shapes=[pltpu.SemaphoreType.DMA((14,)), pltpu.SemaphoreType.DMA((14,))],
        compiler_params=pltpu.CompilerParams(
            collective_id=0, has_side_effects=True, vmem_limit_bytes=GATHER_VMEM
        ),
        name="gather_features",
    )(x_t)


def forward_kernel(coords, live, a_ref, xt_ref, out_ref, xs, acc):
    n_rb = acc.shape[0] - 1
    n_cb = xs.shape[0]
    for c in range(n_cb):
        xs[c] = xt_ref[:, c * 128 : (c + 1) * 128].T

    def clear(i, _):
        acc[i] = jnp.zeros(acc.shape[1:], F32)
        return 0

    lax.fori_loop(0, n_rb, clear, 0)

    def some(q, _):
        products = []
        for u in range(UNROLL):
            s = q * UNROLL + u
            products.append(jnp.dot(a_ref[s], xs[coords[1, s]], preferred_element_type=F32))
        for u in range(UNROLL):
            s = q * UNROLL + u
            r = jnp.where(s < live[0, 0], coords[0, s], n_rb)
            acc[r] += products[u]
        return 0

    lax.fori_loop(0, (live[0, 0] + UNROLL - 1) // UNROLL, some, 0)

    def put(chip, _):
        for k in range(4):
            out_ref[k // 2, chip, (k % 2) * 128 : (k % 2 + 1) * 128, :] = acc[chip * 4 + k].astype(BF16)
        return 0

    lax.fori_loop(0, 16, put, 0)


def forward_products(coords, live, blocks, x_t):
    return pl.pallas_call(
        forward_kernel,
        out_shape=jax.ShapeDtypeStruct((2, 16, 256, 256), BF16),
        in_specs=[SMEM, SMEM, VMEM, VMEM],
        out_specs=VMEM,
        scratch_shapes=[pltpu.VMEM((16, 128, 256), BF16), pltpu.VMEM((65, 128, 256), F32)],
        compiler_params=pltpu.CompilerParams(vmem_limit_bytes=FORWARD_VMEM),
        name="forward_products",
    )(coords, live, blocks, x_t)


def middle_kernel(
    norm, part, cot_ref, w_ref, bias_ref, out_ref, full_ref, all_t,
    r_a, s_a, r_b1l, r_b1r, r_b2l, r_b2r, s_b, r_c,
    term_ref, t_c, u_c, t_y, u_y, t_x, u_x, t_z, sends, recvs,
):
    zh, y, x, zl, core = place()
    right = device(zh, y, rem4(x + 1), zl, core)
    left = device(zh, y, rem4(x + 3), zl, core)
    twin = device(zh, y, x, zl, 1 - core)
    along = [None] + [device(zh, y, x, rem4(zl + k), core) for k in range(1, 4)]
    y_dev = [None] + [device(zh, rem4(y + k), x, zl, core) for k in range(1, 4)]
    x_dev = [None] + [device(zh, y, rem4(x + k), zl, core) for k in range(1, 4)]
    zz = zh * 4 + zl
    z_dev = [None]
    for k in range(1, 8):
        other = lax.rem(zz + k, 8)
        z_dev.append(device(other // 4, y, x, lax.rem(other, 4), core))
    meet([twin] + y_dev[1:] + x_dev[1:] + z_dev[1:])
    started = []
    used = [0]

    def start(src, dst, dev):
        c = copy_to(src, dst, sends, recvs, used[0], dev)
        used[0] += 1
        c.start()
        started.append(c)
        return c

    top, low = pl.ds(0, 128), pl.ds(128, 128)
    xk = [rem4(x + k) for k in range(4)]
    zk = [rem4(zl + k) for k in range(4)]
    order = (1, 2, 3, 0)
    a = {}
    for k in (2, 1, 3, 0):
        sl = pl.ds(xk[k] * 4, 4)
        a[k] = start(part.at[1 - core, sl], r_a.at[sl], twin)

    def add_cores(k):
        a[k].wait_recv()

        def one(z, _):
            i = xk[k] * 4 + z
            s_a[i] = (part[core, i].astype(F32) + r_a[i].astype(F32)).astype(BF16)
            return 0

        lax.fori_loop(0, 4, one, 0)

    add_cores(2)
    b1 = {}
    for k in order:
        i = xk[2] * 4 + zk[k]
        b1[k] = (
            start(s_a.at[i, top], r_b1l.at[k], right),
            start(s_a.at[i, low], r_b1r.at[k], left),
        )
    b2 = {}
    add_cores(1)
    for k in order:
        b2[k] = [start(s_a.at[xk[1] * 4 + zk[k], low], r_b2l.at[k, low], right)]
    add_cores(3)
    for k in order:
        b2[k].append(start(s_a.at[xk[3] * 4 + zk[k], top], r_b2r.at[k, top], left))
    for k in order:
        b1[k][0].wait_recv()
        i = xk[1] * 4 + zk[k]
        s_a[i, top] = (s_a[i, top].astype(F32) + r_b1l[k].astype(F32)).astype(BF16)
        b2[k].append(start(s_a.at[i, top], r_b2l.at[k, top], right))
        b1[k][1].wait_recv()
        j = xk[3] * 4 + zk[k]
        s_a[j, low] = (s_a[j, low].astype(F32) + r_b1r[k].astype(F32)).astype(BF16)
        b2[k].append(start(s_a.at[j, low], r_b2r.at[k, low], left))
    add_cores(0)
    c_z = {}
    total = None
    for k in order:
        for c in b2[k]:
            c.wait_recv()
        i = x * 4 + zk[k]
        value = s_a[i].astype(F32) + (r_b2l[k].astype(F32) + r_b2r[k].astype(F32))
        if k == 0:
            total = value
        else:
            s_b[k] = value.astype(BF16)
            c_z[k] = start(s_b.at[k], r_c.at[k], along[k])
    for k in (1, 2, 3):
        c_z[k].wait_recv()
        total = total + r_c[k].astype(F32)
    aggregate = total.astype(BF16)
    preact = jnp.dot(aggregate, w_ref[...], preferred_element_type=F32) + bias_ref[...]
    sig = jax.nn.sigmoid(preact)
    derivative = sig * (1.0 + preact * (1.0 - sig))
    grad_pre = (cot_ref[...].astype(F32) * derivative).astype(BF16)
    grad_agg = lax.dot_general(
        w_ref[...], grad_pre, (((1,), (1,)), ((), ())), preferred_element_type=F32
    ).astype(BF16)
    mine = (x * 4 + zl) * 2 + core
    full_ref[mine, 0] = grad_agg[:, 0:128]
    full_ref[mine, 1] = grad_agg[:, 128:256]

    def at(xx, zz):
        return (xx * 4 + zz) * 2 + core

    def ring(d):
        here = full_ref
        return (
            start(here.at[d, 0], here.at[d, 0], right),
            start(here.at[d, 1], here.at[d, 1], left),
            start(here.at[d, 1], here.at[d, 1], right),
            start(here.at[d, 0], here.at[d, 0], left),
        )

    def same(d, dev):
        return start(full_ref.at[d], full_ref.at[d], dev)

    def same_half(d, h, dev):
        return start(full_ref.at[d, h], full_ref.at[d, h], dev)

    z_in = {k: same(mine, along[k]) for k in (1, 2, 3)}
    rings = {0: ring(mine)}
    twins = [same(mine, twin)]
    zb = [rem4(zl + 4 - k) for k in range(4)]

    out_ref[...] = (preact * sig).astype(BF16)
    term_ref[:, 0:256] = lax.dot_general(
        aggregate, grad_pre, (((0,), (0,)), ((), ())), preferred_element_type=F32
    )
    term_ref[:, 256:384] = lax.dot_general(
        grad_pre, jnp.ones((256, 128), BF16), (((0,), (0,)), ((), ())), preferred_element_type=F32
    )

    yk = [rem4(y + k) for k in range(4)]

    def parameters():
        def at_row(row, n):
            return pl.ds(pl.multiple_of(row, n), n)

        half = at_row(core * 128, 128)
        c = start(term_ref.at[at_row((1 - core) * 128, 128)], t_c, twin)
        yield
        c.wait_recv()
        u_c[...] = term_ref[half] + t_c[...]
        cs = [start(u_c.at[at_row(yk[k] * 32, 32)], t_y.at[k], y_dev[k]) for k in (2, 1, 3)]
        yield
        for c in cs:
            c.wait_recv()
        u_y[...] = u_c[at_row(y * 32, 32)] + (t_y[1] + t_y[2] + t_y[3])
        cs = [start(u_y.at[at_row(xk[k] * 8, 8)], t_x.at[k], x_dev[k]) for k in (2, 1, 3)]
        yield
        for c in cs:
            c.wait_recv()
        u_x[...] = u_y[at_row(x * 8, 8)] + (t_x[1] + t_x[2] + t_x[3])
        cs = [start(u_x, t_z.at[zz], z_dev[k]) for k in (4, 3, 5, 2, 6, 1, 7)]
        t_z[zz] = u_x[...]
        yield
        for c in cs:
            c.wait_recv()
        value = t_z[0]
        for k in range(1, 8):
            value = value + t_z[k]
        spot = at_row(core * 128 + y * 32 + x * 8, 8)
        all_t[spot] = value * norm
        cs = [start(all_t.at[spot], all_t.at[spot], x_dev[k]) for k in (2, 1, 3)]
        yield
        for c in cs:
            c.wait_recv()
        spot = at_row(core * 128 + y * 32, 32)
        cs = [start(all_t.at[spot], all_t.at[spot], y_dev[k]) for k in (2, 1, 3)]
        yield
        for c in cs:
            c.wait_recv()
        c = start(all_t.at[half], all_t.at[half], twin)
        yield
        c.wait_recv()
        yield

    params = parameters()
    next(params)
    forwards = {}

    def relay(k):
        dl, dr = at(xk[3], zb[k]), at(xk[1], zb[k])
        rings[k][0].wait_recv()
        fr = same_half(dl, 0, right)
        rings[k][1].wait_recv()
        fl = same_half(dr, 1, left)
        forwards[k] = (fr, fl)

    def hand_over(k):
        dl, dr = at(xk[3], zb[k]), at(xk[1], zb[k])
        rings[k][2].wait_recv()
        twins.append(same(dl, twin))
        rings[k][3].wait_recv()
        twins.append(same(dr, twin))

    for k in range(4):
        if k < 3:
            d = at(x, zb[k + 1])
            z_in[k + 1].wait_recv()
            rings[k + 1] = ring(d)
            twins.append(same(d, twin))
        relay(k)
        if k > 0:
            next(params)
        hand_over(k)
        next(params)
    for k in range(4):
        d = at(xk[2], zb[k])
        forwards[k][0].wait_recv()
        twins.append(same_half(d, 0, twin))
        forwards[k][1].wait_recv()
        twins.append(same_half(d, 1, twin))
    for _ in params:
        pass
    for c in twins:
        c.wait_recv()
    for c in started:
        c.wait_send()


def middle(part, cot, weight, bias, norm):
    chunk = (256, 256)
    return pl.pallas_call(
        functools.partial(middle_kernel, norm),
        out_shape=(
            jax.ShapeDtypeStruct(chunk, BF16),
            jax.ShapeDtypeStruct((32, 2, 256, 128), BF16),
            jax.ShapeDtypeStruct((256, 384), F32),
        ),
        in_specs=[VMEM] * 4,
        out_specs=(VMEM,) * 3,
        scratch_shapes=[
            pltpu.VMEM((16,) + chunk, BF16),
            pltpu.VMEM((16,) + chunk, BF16),
            pltpu.VMEM((4, 128, 256), BF16),
            pltpu.VMEM((4, 128, 256), BF16),
            pltpu.VMEM((4,) + chunk, BF16),
            pltpu.VMEM((4,) + chunk, BF16),
            pltpu.VMEM((4,) + chunk, BF16),
            pltpu.VMEM((4,) + chunk, BF16),
            pltpu.VMEM((256, 384), F32),
            pltpu.VMEM((128, 384), F32),
            pltpu.VMEM((128, 384), F32),
            pltpu.VMEM((4, 32, 384), F32),
            pltpu.VMEM((32, 384), F32),
            pltpu.VMEM((4, 8, 384), F32),
            pltpu.VMEM((8, 384), F32),
            pltpu.VMEM((8, 8, 384), F32),
            pltpu.SemaphoreType.DMA((112,)),
            pltpu.SemaphoreType.DMA((112,)),
        ],
        compiler_params=pltpu.CompilerParams(
            collective_id=1, has_side_effects=True, vmem_limit_bytes=MIDDLE_VMEM
        ),
        name="layer",
    )(part, cot, weight, bias)


def backward_kernel(coords, live, a_ref, g_ref, o_ref, t_ref, out_ref, o_out, gw_out, gb_out, acc):
    n_cb = acc.shape[0] - 1
    o_out[...] = o_ref[...]
    gw_out[...] = t_ref[:, 0:256]
    gb_out[...] = t_ref[:, 256:384].T[0:1]

    def clear(i, _):
        acc[i] = jnp.zeros(acc.shape[1:], F32)
        return 0

    lax.fori_loop(0, n_cb, clear, 0)

    def some(q, _):
        products = []
        for u in range(UNROLL):
            s = q * UNROLL + u
            products.append(jnp.dot(g_ref[coords[0, s]], a_ref[s], preferred_element_type=F32))
        for u in range(UNROLL):
            s = q * UNROLL + u
            c = jnp.where(s < live[0, 0], coords[1, s], n_cb)
            acc[c] += products[u]
        return 0

    lax.fori_loop(0, (live[0, 0] + UNROLL - 1) // UNROLL, some, 0)
    for c in range(n_cb):
        out_ref[:, c * 128 : (c + 1) * 128] = acc[c].astype(BF16)


def backward_products(coords, live, blocks, grads, out, term):
    return pl.pallas_call(
        backward_kernel,
        out_shape=(
            jax.ShapeDtypeStruct((256, 2048), BF16),
            jax.ShapeDtypeStruct((256, 256), BF16),
            jax.ShapeDtypeStruct((256, 256), F32),
            jax.ShapeDtypeStruct((1, 256), F32),
        ),
        in_specs=[SMEM, SMEM, VMEM, VMEM, VMEM, VMEM],
        out_specs=(VMEM,) * 4,
        scratch_shapes=[pltpu.VMEM((17, 256, 128), F32)],
        compiler_params=pltpu.CompilerParams(vmem_limit_bytes=BACKWARD_VMEM),
        name="backward_products",
    )(coords, live, blocks, grads, out, term)


def finish_kernel(
    part, gx_ref, r_b1l, r_b1r, s_b1r, s_b1l, r_b2l, r_b2r, s_b, r_c, sends, recvs,
):
    zh, y, x, zl, core = place()
    right = device(zh, rem4(y + 1), x, zl, core)
    left = device(zh, rem4(y + 3), x, zl, core)
    across = device(1 - zh, y, x, zl, core)
    meet((left, right, across))
    started = []
    used = [0]

    def start(src, dst, dev):
        c = copy_to(src, dst, sends, recvs, used[0], dev)
        used[0] += 1
        c.start()
        started.append(c)
        return c

    yk = [rem4(y + k) for k in range(4)]
    top, low = pl.ds(0, 16), pl.ds(16, 16)

    zs = (1 - zh, zh)
    b1, b2 = [], []

    def first(j):
        i = zs[j] * 4 + yk[2]
        b1.append(
            (start(part.at[i, top], r_b1l.at[j], right), start(part.at[i, low], r_b1r.at[j], left))
        )

    def plain(j):
        b2.append(
            [
                start(part.at[zs[j] * 4 + yk[1], low], r_b2l.at[j, low], right),
                start(part.at[zs[j] * 4 + yk[3], top], r_b2r.at[j, top], left),
            ]
        )

    def added(j):
        b1[j][0].wait_recv()
        s_b1r[j] = (part[zs[j] * 4 + yk[1], top].astype(F32) + r_b1l[j].astype(F32)).astype(BF16)
        b2[j].append(start(s_b1r.at[j], r_b2l.at[j, top], right))
        b1[j][1].wait_recv()
        s_b1l[j] = (part[zs[j] * 4 + yk[3], low].astype(F32) + r_b1r[j].astype(F32)).astype(BF16)
        b2[j].append(start(s_b1l.at[j], r_b2r.at[j, low], left))

    first(0)
    plain(0)
    first(1)
    added(0)
    plain(1)
    added(1)

    def summed(j):
        for c in b2[j]:
            c.wait_recv()
        return part[zs[j] * 4 + y].astype(F32) + (r_b2l[j].astype(F32) + r_b2r[j].astype(F32))

    s_b[...] = summed(0).astype(BF16)
    cz = start(s_b, r_c, across)
    own = summed(1)
    cz.wait_recv()
    gx_ref[...] = (own + r_c[...].astype(F32)).astype(BF16)
    for c in started:
        c.wait_send()


def finish(part):
    half, whole = (2, 16, 2048), (2, 32, 2048)
    return pl.pallas_call(
        finish_kernel,
        out_shape=jax.ShapeDtypeStruct((32, 2048), BF16),
        in_specs=[VMEM],
        out_specs=VMEM,
        scratch_shapes=[
            pltpu.VMEM(half, BF16),
            pltpu.VMEM(half, BF16),
            pltpu.VMEM(half, BF16),
            pltpu.VMEM(half, BF16),
            pltpu.VMEM(whole, BF16),
            pltpu.VMEM(whole, BF16),
            pltpu.VMEM(whole[1:], BF16),
            pltpu.VMEM(whole[1:], BF16),
            pltpu.SemaphoreType.DMA((16,)),
            pltpu.SemaphoreType.DMA((16,)),
        ],
        compiler_params=pltpu.CompilerParams(
            collective_id=2, has_side_effects=True, vmem_limit_bytes=FINISH_VMEM
        ),
        name="finish",
    )(part)


def on_device(features, block_values, block_coords, live_blocks, weight, bias, cotangent):
    blocks, coords = block_values[0, 0], block_coords[0, 0]
    nodes = features.shape[0] * lax.axis_size("col")
    x_t = gather_rows(features.T).reshape(256, 2048)
    part = forward_products(coords, live_blocks, blocks, x_t)
    out, grads, term = middle(part, cotangent, weight, bias[None], nodes**-0.5)
    part_x, out, grad_weight, grad_bias = backward_products(
        coords, live_blocks, blocks, grads.reshape(64, 256, 128), out, term
    )
    gx_t = finish(part_x.reshape(8, 32, 2048))
    return out, gx_t.T, grad_weight, grad_bias[0]


def solution(mesh):
    in_specs = (
        P("col", "row"),
        P("row", "col", None, None, None),
        P("row", "col", None, None),
        P("row", "col"),
        P(),
        P(),
        P(("row", "col"), None),
    )
    out_specs = (P(("row", "col"), None), P("col", "row"), P(), P())
    return jax.shard_map(
        on_device, mesh=mesh, in_specs=in_specs, out_specs=out_specs, check_vma=False
    )
```

```python
import functools

import jax
import jax.numpy as jnp
from jax import lax
from jax.experimental import pallas as pl
from jax.experimental.pallas import tpu as pltpu
from jax.sharding import PartitionSpec as P

MESH = pl.DeviceIdType.MESH
F32 = jnp.float32
BF16 = jnp.bfloat16
UNROLL = 8
VMEM = pl.BlockSpec(memory_space=pltpu.VMEM)
SMEM = pl.BlockSpec(memory_space=pltpu.SMEM)
ANY = pl.BlockSpec(memory_space=pltpu.HBM)
MIB = 2**20
GATHER_VMEM = 42 * MIB
FORWARD_VMEM = 24 * MIB
MIDDLE_VMEM = 24 * MIB
BACKWARD_VMEM = 20 * MIB
FINISH_VMEM = 6 * MIB


def place():
    row, col = lax.axis_index("row"), lax.axis_index("col")
    return row // 4, row % 4, col // 8, (col // 2) % 4, col % 2


def device(zh, y, x, zl, core):
    return (zh * 4 + y, (x * 4 + zl) * 2 + core)


def copy_to(src, dst, sends, recvs, at, dev):
    return pltpu.make_async_remote_copy(
        src_ref=src,
        dst_ref=dst,
        send_sem=sends.at[at],
        recv_sem=recvs.at[at],
        device_id=dev,
        device_id_type=MESH,
    )


def meet(devices):
    barrier = pltpu.get_barrier_semaphore()
    for dev in devices:
        pl.semaphore_signal(barrier, inc=1, device_id=dev, device_id_type=MESH)
    pl.semaphore_wait(barrier, len(devices))


def rem4(v):
    return lax.rem(v, 4)


def gather_rows_kernel(x_ref, b_ref, c_ref, full_ref, b_out, c_out, sends, recvs, locals_):
    zh, y, x, zl, core = place()
    right = device(zh, rem4(y + 1), x, zl, core)
    left = device(zh, rem4(y + 3), x, zl, core)
    across = device(1 - zh, y, x, zl, core)
    meet((left, right, across))
    mine = zh * 4 + y
    other = (1 - zh) * 4 + y
    staged = [
        pltpu.make_async_copy(src, dst, locals_.at[i])
        for i, (src, dst) in enumerate(((x_ref, full_ref.at[mine]), (b_ref, b_out), (c_ref, c_out)))
    ]
    halves = (pl.ds(0, 16), pl.ds(16, 16))
    started = []

    def start(c):
        c.start()
        started.append(c)
        return c

    zc = [
        start(copy_to(x_ref.at[h], full_ref.at[mine, h], sends, recvs, 12 + i, across))
        for i, h in enumerate(halves)
    ]
    firsts = []
    for k in range(2):
        me = mine if k == 0 else other
        base = (zh if k == 0 else 1 - zh) * 4
        src = x_ref if k == 0 else full_ref.at[other]

        def ring(h, at, dev):
            return start(
                copy_to(src.at[halves[h]], full_ref.at[me, halves[h]], sends, recvs, k * 6 + at, dev)
            )

        if k == 1:
            zc[0].wait_recv()
        r0 = ring(0, 0, right)
        if k == 1:
            zc[1].wait_recv()
        l1 = ring(1, 1, left)
        r1 = ring(1, 2, right)
        l0 = ring(0, 3, left)
        firsts.append((r0, l1, r1, l0, base))
        if k == 0:
            for c in staged:
                c.start()
    forwards = []
    for k in range(2):
        r0, l1, r1, l0, base = firsts[k]
        from_left = base + rem4(y + 3)
        from_right = base + rem4(y + 1)
        r0.wait_recv()
        fr = start(
            copy_to(
                full_ref.at[from_left, halves[0]],
                full_ref.at[from_left, halves[0]],
                sends,
                recvs,
                k * 6 + 4,
                right,
            )
        )
        l1.wait_recv()
        fl = start(
            copy_to(
                full_ref.at[from_right, halves[1]],
                full_ref.at[from_right, halves[1]],
                sends,
                recvs,
                k * 6 + 5,
                left,
            )
        )
        forwards += [r1, l0, fr, fl]
    for c in forwards:
        c.wait_recv()
    for c in staged:
        c.wait()
    for c in started:
        c.wait_send()


def gather_rows(x_t, blocks, coords):
    width, verts = x_t.shape
    return pl.pallas_call(
        gather_rows_kernel,
        out_shape=(
            jax.ShapeDtypeStruct((8, width, verts), BF16),
            jax.ShapeDtypeStruct(blocks.shape, BF16),
            jax.ShapeDtypeStruct(coords.shape, jnp.int32),
        ),
        in_specs=[ANY] * 3,
        out_specs=(VMEM,) * 3,
        scratch_shapes=[
            pltpu.SemaphoreType.DMA((14,)),
            pltpu.SemaphoreType.DMA((14,)),
            pltpu.SemaphoreType.DMA((3,)),
        ],
        compiler_params=pltpu.CompilerParams(
            collective_id=0, has_side_effects=True, vmem_limit_bytes=GATHER_VMEM
        ),
        name="gather_features",
    )(x_t, blocks, coords)


def forward_kernel(coords, live, a_ref, xt_ref, out_ref, xs, acc):
    n_rb = acc.shape[0] - 1
    n_cb = xs.shape[0]
    for c in range(n_cb):
        xs[c] = xt_ref[:, c * 128 : (c + 1) * 128].T

    def clear(i, _):
        acc[i] = jnp.zeros(acc.shape[1:], F32)
        return 0

    lax.fori_loop(0, n_rb, clear, 0)

    def some(q, _):
        products = []
        for u in range(UNROLL):
            s = q * UNROLL + u
            products.append(jnp.dot(a_ref[s], xs[coords[1, s]], preferred_element_type=F32))
        for u in range(UNROLL):
            s = q * UNROLL + u
            r = jnp.where(s < live[0, 0], coords[0, s], n_rb)
            acc[r] += products[u]
        return 0

    lax.fori_loop(0, (live[0, 0] + UNROLL - 1) // UNROLL, some, 0)

    def put(chip, _):
        for k in range(4):
            out_ref[k // 2, chip, (k % 2) * 128 : (k % 2 + 1) * 128, :] = acc[chip * 4 + k].astype(BF16)
        return 0

    lax.fori_loop(0, 16, put, 0)


def forward_products(coords, live, blocks, x_t):
    return pl.pallas_call(
        forward_kernel,
        out_shape=jax.ShapeDtypeStruct((2, 16, 256, 256), BF16),
        in_specs=[SMEM, SMEM, VMEM, VMEM],
        out_specs=VMEM,
        scratch_shapes=[pltpu.VMEM((16, 128, 256), BF16), pltpu.VMEM((65, 128, 256), F32)],
        compiler_params=pltpu.CompilerParams(vmem_limit_bytes=FORWARD_VMEM),
        name="forward_products",
    )(coords, live, blocks, x_t)


def middle_kernel(
    norm, part, cot_ref, w_ref, bias_ref, out_ref, full_ref, all_t,
    r_a, s_a, r_b1l, r_b1r, r_b2l, r_b2r, s_b, r_c,
    term_ref, t_c, u_c, t_y, u_y, t_x, u_x, t_z, sends, recvs,
):
    zh, y, x, zl, core = place()
    right = device(zh, y, rem4(x + 1), zl, core)
    left = device(zh, y, rem4(x + 3), zl, core)
    twin = device(zh, y, x, zl, 1 - core)
    along = [None] + [device(zh, y, x, rem4(zl + k), core) for k in range(1, 4)]
    y_dev = [None] + [device(zh, rem4(y + k), x, zl, core) for k in range(1, 4)]
    x_dev = [None] + [device(zh, y, rem4(x + k), zl, core) for k in range(1, 4)]
    zz = zh * 4 + zl
    z_dev = [None]
    for k in range(1, 8):
        other = lax.rem(zz + k, 8)
        z_dev.append(device(other // 4, y, x, lax.rem(other, 4), core))
    meet([twin] + y_dev[1:] + x_dev[1:] + z_dev[1:])
    started = []
    used = [0]

    def start(src, dst, dev):
        c = copy_to(src, dst, sends, recvs, used[0], dev)
        used[0] += 1
        c.start()
        started.append(c)
        return c

    top, low = pl.ds(0, 128), pl.ds(128, 128)
    xk = [rem4(x + k) for k in range(4)]
    zk = [rem4(zl + k) for k in range(4)]
    order = (2, 1, 3, 0)
    a = {}
    for k in (2, 1, 3, 0):
        sl = pl.ds(xk[k] * 4, 4)
        a[k] = start(part.at[1 - core, sl], r_a.at[sl], twin)

    def add_cores(k):
        a[k].wait_recv()

        def one(z, _):
            i = xk[k] * 4 + z
            s_a[i] = (part[core, i].astype(F32) + r_a[i].astype(F32)).astype(BF16)
            return 0

        lax.fori_loop(0, 4, one, 0)

    b1, b2, c_z = {}, {}, {}

    def first(k):
        i = xk[2] * 4 + zk[k]
        b1[k] = (
            start(s_a.at[i, top], r_b1l.at[k], right),
            start(s_a.at[i, low], r_b1r.at[k], left),
        )

    def plain(k):
        b2[k] = [
            start(s_a.at[xk[1] * 4 + zk[k], low], r_b2l.at[k, low], right),
            start(s_a.at[xk[3] * 4 + zk[k], top], r_b2r.at[k, top], left),
        ]

    def added(k):
        b1[k][0].wait_recv()
        i = xk[1] * 4 + zk[k]
        s_a[i, top] = (s_a[i, top].astype(F32) + r_b1l[k].astype(F32)).astype(BF16)
        b2[k].append(start(s_a.at[i, top], r_b2l.at[k, top], right))
        b1[k][1].wait_recv()
        j = xk[3] * 4 + zk[k]
        s_a[j, low] = (s_a[j, low].astype(F32) + r_b1r[k].astype(F32)).astype(BF16)
        b2[k].append(start(s_a.at[j, low], r_b2r.at[k, low], left))

    def summed(k):
        for c in b2[k]:
            c.wait_recv()
        i = x * 4 + zk[k]
        return s_a[i].astype(F32) + (r_b2l[k].astype(F32) + r_b2r[k].astype(F32))

    def along_z(k):
        s_b[k] = summed(k).astype(BF16)
        c_z[k] = start(s_b.at[k], r_c.at[k], along[k])

    add_cores(2)
    first(order[0])
    first(order[1])
    add_cores(1)
    add_cores(3)
    plain(order[0])
    for n in range(4):
        added(order[n])
        if n < 2:
            first(order[n + 2])
        if n < 3:
            plain(order[n + 1])
        if n == 0:
            add_cores(0)
        else:
            along_z(order[n - 1])
    total = summed(0)
    for k in (1, 2, 3):
        c_z[k].wait_recv()
        total = total + r_c[k].astype(F32)
    aggregate = total.astype(BF16)
    preact = jnp.dot(aggregate, w_ref[...], preferred_element_type=F32) + bias_ref[...]
    sig = jax.nn.sigmoid(preact)
    derivative = sig * (1.0 + preact * (1.0 - sig))
    grad_pre = (cot_ref[...].astype(F32) * derivative).astype(BF16)
    grad_agg = lax.dot_general(
        w_ref[...], grad_pre, (((1,), (1,)), ((), ())), preferred_element_type=F32
    ).astype(BF16)
    mine = (x * 4 + zl) * 2 + core
    full_ref[mine, 0] = grad_agg[:, 0:128]
    full_ref[mine, 1] = grad_agg[:, 128:256]

    def at(xx, zz):
        return (xx * 4 + zz) * 2 + core

    def ring(d):
        here = full_ref
        return (
            start(here.at[d, 0], here.at[d, 0], right),
            start(here.at[d, 1], here.at[d, 1], left),
            start(here.at[d, 1], here.at[d, 1], right),
            start(here.at[d, 0], here.at[d, 0], left),
        )

    def same(d, dev):
        return start(full_ref.at[d], full_ref.at[d], dev)

    def same_half(d, h, dev):
        return start(full_ref.at[d, h], full_ref.at[d, h], dev)

    z_in = {k: same(mine, along[k]) for k in (1, 2, 3)}
    rings = {0: ring(mine)}
    twins = [same(mine, twin)]
    zb = [rem4(zl + 4 - k) for k in range(4)]

    out_ref[...] = (preact * sig).astype(BF16)
    term_ref[:, 0:256] = lax.dot_general(
        aggregate, grad_pre, (((0,), (0,)), ((), ())), preferred_element_type=F32
    )
    term_ref[:, 256:384] = lax.dot_general(
        grad_pre, jnp.ones((256, 128), BF16), (((0,), (0,)), ((), ())), preferred_element_type=F32
    )

    yk = [rem4(y + k) for k in range(4)]

    def parameters():
        def at_row(row, n):
            return pl.ds(pl.multiple_of(row, n), n)

        half = at_row(core * 128, 128)
        c = start(term_ref.at[at_row((1 - core) * 128, 128)], t_c, twin)
        yield
        c.wait_recv()
        u_c[...] = term_ref[half] + t_c[...]
        cs = [start(u_c.at[at_row(yk[k] * 32, 32)], t_y.at[k], y_dev[k]) for k in (2, 1, 3)]
        yield
        for c in cs:
            c.wait_recv()
        u_y[...] = u_c[at_row(y * 32, 32)] + (t_y[1] + t_y[2] + t_y[3])
        cs = [start(u_y.at[at_row(xk[k] * 8, 8)], t_x.at[k], x_dev[k]) for k in (2, 1, 3)]
        yield
        for c in cs:
            c.wait_recv()
        u_x[...] = u_y[at_row(x * 8, 8)] + (t_x[1] + t_x[2] + t_x[3])
        cs = [start(u_x, t_z.at[zz], z_dev[k]) for k in (4, 3, 5, 2, 6, 1, 7)]
        t_z[zz] = u_x[...]
        yield
        for c in cs:
            c.wait_recv()
        value = t_z[0]
        for k in range(1, 8):
            value = value + t_z[k]
        spot = at_row(core * 128 + y * 32 + x * 8, 8)
        all_t[spot] = value * norm
        cs = [start(all_t.at[spot], all_t.at[spot], x_dev[k]) for k in (2, 1, 3)]
        yield
        for c in cs:
            c.wait_recv()
        spot = at_row(core * 128 + y * 32, 32)
        cs = [start(all_t.at[spot], all_t.at[spot], y_dev[k]) for k in (2, 1, 3)]
        yield
        for c in cs:
            c.wait_recv()
        c = start(all_t.at[half], all_t.at[half], twin)
        yield
        c.wait_recv()
        yield

    params = parameters()
    next(params)
    forwards = {}

    def relay(k):
        dl, dr = at(xk[3], zb[k]), at(xk[1], zb[k])
        rings[k][0].wait_recv()
        fr = same_half(dl, 0, right)
        rings[k][1].wait_recv()
        fl = same_half(dr, 1, left)
        forwards[k] = (fr, fl)

    def hand_over(k):
        dl, dr = at(xk[3], zb[k]), at(xk[1], zb[k])
        rings[k][2].wait_recv()
        twins.append(same(dl, twin))
        rings[k][3].wait_recv()
        twins.append(same(dr, twin))

    for k in range(4):
        relay(k)
        if k == 1:
            next(params)
        hand_over(k)
        if k > 0:
            next(params)
        if k < 3:
            d = at(x, zb[k + 1])
            z_in[k + 1].wait_recv()
            rings[k + 1] = ring(d)
            twins.append(same(d, twin))
        if k == 0:
            next(params)
    for k in range(4):
        if k == 3:
            next(params)
        d = at(xk[2], zb[k])
        forwards[k][0].wait_recv()
        twins.append(same_half(d, 0, twin))
        forwards[k][1].wait_recv()
        twins.append(same_half(d, 1, twin))
    for _ in params:
        pass
    for c in twins:
        c.wait_recv()
    for c in started:
        c.wait_send()


def middle(part, cot, weight, bias, norm):
    chunk = (256, 256)
    return pl.pallas_call(
        functools.partial(middle_kernel, norm),
        out_shape=(
            jax.ShapeDtypeStruct(chunk, BF16),
            jax.ShapeDtypeStruct((32, 2, 256, 128), BF16),
            jax.ShapeDtypeStruct((256, 384), F32),
        ),
        in_specs=[VMEM] * 4,
        out_specs=(VMEM,) * 3,
        scratch_shapes=[
            pltpu.VMEM((16,) + chunk, BF16),
            pltpu.VMEM((16,) + chunk, BF16),
            pltpu.VMEM((4, 128, 256), BF16),
            pltpu.VMEM((4, 128, 256), BF16),
            pltpu.VMEM((4,) + chunk, BF16),
            pltpu.VMEM((4,) + chunk, BF16),
            pltpu.VMEM((4,) + chunk, BF16),
            pltpu.VMEM((4,) + chunk, BF16),
            pltpu.VMEM((256, 384), F32),
            pltpu.VMEM((128, 384), F32),
            pltpu.VMEM((128, 384), F32),
            pltpu.VMEM((4, 32, 384), F32),
            pltpu.VMEM((32, 384), F32),
            pltpu.VMEM((4, 8, 384), F32),
            pltpu.VMEM((8, 384), F32),
            pltpu.VMEM((8, 8, 384), F32),
            pltpu.SemaphoreType.DMA((112,)),
            pltpu.SemaphoreType.DMA((112,)),
        ],
        compiler_params=pltpu.CompilerParams(
            collective_id=1, has_side_effects=True, vmem_limit_bytes=MIDDLE_VMEM
        ),
        name="layer",
    )(part, cot, weight, bias)


def backward_kernel(coords, live, a_ref, g_ref, o_ref, t_ref, out_ref, o_out, gw_out, gb_out, acc):
    n_cb = acc.shape[0] - 1
    o_out[...] = o_ref[...]
    gw_out[...] = t_ref[:, 0:256]
    gb_out[...] = t_ref[:, 256:384].T[0:1]

    def clear(i, _):
        acc[i] = jnp.zeros(acc.shape[1:], F32)
        return 0

    lax.fori_loop(0, n_cb, clear, 0)

    def some(q, _):
        products = []
        for u in range(UNROLL):
            s = q * UNROLL + u
            products.append(jnp.dot(g_ref[coords[0, s]], a_ref[s], preferred_element_type=F32))
        for u in range(UNROLL):
            s = q * UNROLL + u
            c = jnp.where(s < live[0, 0], coords[1, s], n_cb)
            acc[c] += products[u]
        return 0

    lax.fori_loop(0, (live[0, 0] + UNROLL - 1) // UNROLL, some, 0)
    for c in range(n_cb):
        out_ref[:, c * 128 : (c + 1) * 128] = acc[c].astype(BF16)


def backward_products(coords, live, blocks, grads, out, term):
    return pl.pallas_call(
        backward_kernel,
        out_shape=(
            jax.ShapeDtypeStruct((256, 2048), BF16),
            jax.ShapeDtypeStruct((256, 256), BF16),
            jax.ShapeDtypeStruct((256, 256), F32),
            jax.ShapeDtypeStruct((1, 256), F32),
        ),
        in_specs=[SMEM, SMEM, VMEM, VMEM, VMEM, VMEM],
        out_specs=(VMEM,) * 4,
        scratch_shapes=[pltpu.VMEM((17, 256, 128), F32)],
        compiler_params=pltpu.CompilerParams(vmem_limit_bytes=BACKWARD_VMEM),
        name="backward_products",
    )(coords, live, blocks, grads, out, term)


def finish_kernel(
    part, gx_ref, r_b1l, r_b1r, s_b1r, s_b1l, r_b2l, r_b2r, s_b, r_c, sends, recvs,
):
    zh, y, x, zl, core = place()
    right = device(zh, rem4(y + 1), x, zl, core)
    left = device(zh, rem4(y + 3), x, zl, core)
    across = device(1 - zh, y, x, zl, core)
    meet((left, right, across))
    started = []
    used = [0]

    def start(src, dst, dev):
        c = copy_to(src, dst, sends, recvs, used[0], dev)
        used[0] += 1
        c.start()
        started.append(c)
        return c

    yk = [rem4(y + k) for k in range(4)]
    top, low = pl.ds(0, 16), pl.ds(16, 16)

    zs = (1 - zh, zh)
    b1, b2 = [], []

    def first(j):
        i = zs[j] * 4 + yk[2]
        b1.append(
            (start(part.at[i, top], r_b1l.at[j], right), start(part.at[i, low], r_b1r.at[j], left))
        )

    def plain(j):
        b2.append(
            [
                start(part.at[zs[j] * 4 + yk[1], low], r_b2l.at[j, low], right),
                start(part.at[zs[j] * 4 + yk[3], top], r_b2r.at[j, top], left),
            ]
        )

    def added(j):
        b1[j][0].wait_recv()
        s_b1r[j] = (part[zs[j] * 4 + yk[1], top].astype(F32) + r_b1l[j].astype(F32)).astype(BF16)
        b2[j].append(start(s_b1r.at[j], r_b2l.at[j, top], right))
        b1[j][1].wait_recv()
        s_b1l[j] = (part[zs[j] * 4 + yk[3], low].astype(F32) + r_b1r[j].astype(F32)).astype(BF16)
        b2[j].append(start(s_b1l.at[j], r_b2r.at[j, low], left))

    for j in range(2):
        first(j)
        plain(j)
        added(j)

    def summed(j):
        for c in b2[j]:
            c.wait_recv()
        return part[zs[j] * 4 + y].astype(F32) + (r_b2l[j].astype(F32) + r_b2r[j].astype(F32))

    s_b[...] = summed(0).astype(BF16)
    cz = start(s_b, r_c, across)
    own = summed(1)
    cz.wait_recv()
    gx_ref[...] = (own + r_c[...].astype(F32)).astype(BF16)
    for c in started:
        c.wait_send()


def finish(part):
    half, whole = (2, 16, 2048), (2, 32, 2048)
    return pl.pallas_call(
        finish_kernel,
        out_shape=jax.ShapeDtypeStruct((32, 2048), BF16),
        in_specs=[VMEM],
        out_specs=VMEM,
        scratch_shapes=[
            pltpu.VMEM(half, BF16),
            pltpu.VMEM(half, BF16),
            pltpu.VMEM(half, BF16),
            pltpu.VMEM(half, BF16),
            pltpu.VMEM(whole, BF16),
            pltpu.VMEM(whole, BF16),
            pltpu.VMEM(whole[1:], BF16),
            pltpu.VMEM(whole[1:], BF16),
            pltpu.SemaphoreType.DMA((16,)),
            pltpu.SemaphoreType.DMA((16,)),
        ],
        compiler_params=pltpu.CompilerParams(
            collective_id=2, has_side_effects=True, vmem_limit_bytes=FINISH_VMEM
        ),
        name="finish",
    )(part)


def on_device(features, block_values, block_coords, live_blocks, weight, bias, cotangent):
    blocks, coords = block_values[0, 0], block_coords[0, 0]
    nodes = features.shape[0] * lax.axis_size("col")
    x_t, blocks, coords = gather_rows(features.T, blocks, coords)
    part = forward_products(coords, live_blocks, blocks, x_t.reshape(256, 2048))
    out, grads, term = middle(part, cotangent, weight, bias[None], nodes**-0.5)
    part_x, out, grad_weight, grad_bias = backward_products(
        coords, live_blocks, blocks, grads.reshape(64, 256, 128), out, term
    )
    gx_t = finish(part_x.reshape(8, 32, 2048))
    return out, gx_t.T, grad_weight, grad_bias[0]


def solution(mesh):
    in_specs = (
        P("col", "row"),
        P("row", "col", None, None, None),
        P("row", "col", None, None),
        P("row", "col"),
        P(),
        P(),
        P(("row", "col"), None),
    )
    out_specs = (P(("row", "col"), None), P("col", "row"), P(), P())
    return jax.shard_map(
        on_device, mesh=mesh, in_specs=in_specs, out_specs=out_specs, check_vma=False
    )
```

```python
import functools

import jax
import jax.numpy as jnp
from jax import lax
from jax.experimental import pallas as pl
from jax.experimental.pallas import tpu as pltpu
from jax.sharding import PartitionSpec as P

MESH = pl.DeviceIdType.MESH
F32 = jnp.float32
BF16 = jnp.bfloat16
UNROLL = 16
VMEM = pl.BlockSpec(memory_space=pltpu.VMEM)
SMEM = pl.BlockSpec(memory_space=pltpu.SMEM)
ANY = pl.BlockSpec(memory_space=pltpu.HBM)
MIB = 2**20
GATHER_VMEM = 42 * MIB
FORWARD_VMEM = 24 * MIB
MIDDLE_VMEM = 24 * MIB
BACKWARD_VMEM = 20 * MIB
FINISH_VMEM = 6 * MIB


def place():
    row, col = lax.axis_index("row"), lax.axis_index("col")
    return row // 4, row % 4, col // 8, (col // 2) % 4, col % 2


def device(zh, y, x, zl, core):
    return (zh * 4 + y, (x * 4 + zl) * 2 + core)


def copy_to(src, dst, sends, recvs, at, dev):
    return pltpu.make_async_remote_copy(
        src_ref=src,
        dst_ref=dst,
        send_sem=sends.at[at],
        recv_sem=recvs.at[at],
        device_id=dev,
        device_id_type=MESH,
    )


def meet(devices):
    barrier = pltpu.get_barrier_semaphore()
    for dev in devices:
        pl.semaphore_signal(barrier, inc=1, device_id=dev, device_id_type=MESH)
    pl.semaphore_wait(barrier, len(devices))


def rem4(v):
    return lax.rem(v, 4)


def gather_rows_kernel(x_ref, b_ref, c_ref, full_ref, b_out, c_out, sends, recvs, locals_):
    zh, y, x, zl, core = place()
    right = device(zh, rem4(y + 1), x, zl, core)
    left = device(zh, rem4(y + 3), x, zl, core)
    across = device(1 - zh, y, x, zl, core)
    meet((left, right, across))
    mine = zh * 4 + y
    other = (1 - zh) * 4 + y
    staged = [
        pltpu.make_async_copy(src, dst, locals_.at[i])
        for i, (src, dst) in enumerate(((x_ref, full_ref.at[mine]), (b_ref, b_out), (c_ref, c_out)))
    ]
    halves = (pl.ds(0, 16), pl.ds(16, 16))
    started = []

    def start(c):
        c.start()
        started.append(c)
        return c

    zc = [
        start(copy_to(x_ref.at[h], full_ref.at[mine, h], sends, recvs, 12 + i, across))
        for i, h in enumerate(halves)
    ]
    forwards = []
    for k in range(2):
        me = mine if k == 0 else other
        base = (zh if k == 0 else 1 - zh) * 4
        src = x_ref if k == 0 else full_ref.at[other]

        def ring(h, at, dev):
            return start(
                copy_to(src.at[halves[h]], full_ref.at[me, halves[h]], sends, recvs, k * 6 + at, dev)
            )

        if k == 1:
            zc[0].wait_recv()
        r0 = ring(0, 0, right)
        if k == 1:
            zc[1].wait_recv()
        l1 = ring(1, 1, left)
        r1 = ring(1, 2, right)
        l0 = ring(0, 3, left)
        if k == 0:
            for c in staged:
                c.start()
        from_left = base + rem4(y + 3)
        from_right = base + rem4(y + 1)
        r0.wait_recv()
        fr = start(
            copy_to(
                full_ref.at[from_left, halves[0]],
                full_ref.at[from_left, halves[0]],
                sends,
                recvs,
                k * 6 + 4,
                right,
            )
        )
        l1.wait_recv()
        fl = start(
            copy_to(
                full_ref.at[from_right, halves[1]],
                full_ref.at[from_right, halves[1]],
                sends,
                recvs,
                k * 6 + 5,
                left,
            )
        )
        forwards += [r1, l0, fr, fl]
    for c in forwards:
        c.wait_recv()
    for c in staged:
        c.wait()
    for c in started:
        c.wait_send()


def gather_rows(x_t, blocks, coords):
    width, verts = x_t.shape
    return pl.pallas_call(
        gather_rows_kernel,
        out_shape=(
            jax.ShapeDtypeStruct((8, width, verts), BF16),
            jax.ShapeDtypeStruct(blocks.shape, BF16),
            jax.ShapeDtypeStruct(coords.shape, jnp.int32),
        ),
        in_specs=[ANY] * 3,
        out_specs=(VMEM,) * 3,
        scratch_shapes=[
            pltpu.SemaphoreType.DMA((14,)),
            pltpu.SemaphoreType.DMA((14,)),
            pltpu.SemaphoreType.DMA((3,)),
        ],
        compiler_params=pltpu.CompilerParams(
            collective_id=0, has_side_effects=True, vmem_limit_bytes=GATHER_VMEM
        ),
        name="gather_features",
    )(x_t, blocks, coords)


def forward_kernel(coords, live, a_ref, xt_ref, out_ref, xs, acc):
    n_rb = acc.shape[0] - 1
    n_cb = xs.shape[0]
    for c in range(n_cb):
        xs[c] = xt_ref[:, c * 128 : (c + 1) * 128].T

    def clear(i, _):
        acc[i] = jnp.zeros(acc.shape[1:], F32)
        return 0

    lax.fori_loop(0, n_rb, clear, 0)

    def some(q, _):
        products = []
        for u in range(UNROLL):
            s = q * UNROLL + u
            products.append(jnp.dot(a_ref[s], xs[coords[1, s]], preferred_element_type=F32))
        for u in range(UNROLL):
            s = q * UNROLL + u
            r = jnp.where(s < live[0, 0], coords[0, s], n_rb)
            acc[r] += products[u]
        return 0

    lax.fori_loop(0, (live[0, 0] + UNROLL - 1) // UNROLL, some, 0)

    def put(chip, _):
        for k in range(4):
            out_ref[k // 2, chip, (k % 2) * 128 : (k % 2 + 1) * 128, :] = acc[chip * 4 + k].astype(BF16)
        return 0

    lax.fori_loop(0, 16, put, 0)


def forward_products(coords, live, blocks, x_t):
    return pl.pallas_call(
        forward_kernel,
        out_shape=jax.ShapeDtypeStruct((2, 16, 256, 256), BF16),
        in_specs=[SMEM, SMEM, VMEM, VMEM],
        out_specs=VMEM,
        scratch_shapes=[pltpu.VMEM((16, 128, 256), BF16), pltpu.VMEM((65, 128, 256), F32)],
        compiler_params=pltpu.CompilerParams(vmem_limit_bytes=FORWARD_VMEM),
        name="forward_products",
    )(coords, live, blocks, x_t)


def middle_kernel(
    norm, part, cot_ref, w_ref, bias_ref, out_ref, full_ref, all_t,
    r_a, s_a, r_b1l, r_b1r, r_b2l, r_b2r, s_b, r_c,
    term_ref, t_c, u_c, t_y, u_y, t_x, u_x, t_z, sends, recvs,
):
    zh, y, x, zl, core = place()
    right = device(zh, y, rem4(x + 1), zl, core)
    left = device(zh, y, rem4(x + 3), zl, core)
    twin = device(zh, y, x, zl, 1 - core)
    along = [None] + [device(zh, y, x, rem4(zl + k), core) for k in range(1, 4)]
    y_dev = [None] + [device(zh, rem4(y + k), x, zl, core) for k in range(1, 4)]
    x_dev = [None] + [device(zh, y, rem4(x + k), zl, core) for k in range(1, 4)]
    zz = zh * 4 + zl
    z_dev = [None]
    for k in range(1, 8):
        other = lax.rem(zz + k, 8)
        z_dev.append(device(other // 4, y, x, lax.rem(other, 4), core))
    meet([twin] + y_dev[1:] + x_dev[1:] + z_dev[1:])
    started = []
    used = [0]

    def start(src, dst, dev):
        c = copy_to(src, dst, sends, recvs, used[0], dev)
        used[0] += 1
        c.start()
        started.append(c)
        return c

    top, low = pl.ds(0, 128), pl.ds(128, 128)
    xk = [rem4(x + k) for k in range(4)]
    zk = [rem4(zl + k) for k in range(4)]
    order = (2, 1, 3, 0)
    a = {}
    far = {}
    for k in order:
        i = xk[2] * 4 + zk[k]
        far[k] = start(part.at[1 - core, i], r_a.at[i], twin)
    for k in (1, 3, 0):
        sl = pl.ds(xk[k] * 4, 4)
        a[k] = start(part.at[1 - core, sl], r_a.at[sl], twin)

    def add_cores(k):
        a[k].wait_recv()

        def one(z, _):
            i = xk[k] * 4 + z
            s_a[i] = (part[core, i].astype(F32) + r_a[i].astype(F32)).astype(BF16)
            return 0

        lax.fori_loop(0, 4, one, 0)

    b1, b2, c_z = {}, {}, {}

    def first(k):
        i = xk[2] * 4 + zk[k]
        far[k].wait_recv()
        s_a[i] = (part[core, i].astype(F32) + r_a[i].astype(F32)).astype(BF16)
        b1[k] = (
            start(s_a.at[i, top], r_b1l.at[k], right),
            start(s_a.at[i, low], r_b1r.at[k], left),
        )

    def plain(k):
        b2[k] = [
            start(s_a.at[xk[1] * 4 + zk[k], low], r_b2l.at[k, low], right),
            start(s_a.at[xk[3] * 4 + zk[k], top], r_b2r.at[k, top], left),
        ]

    def added(k):
        b1[k][0].wait_recv()
        i = xk[1] * 4 + zk[k]
        s_a[i, top] = (s_a[i, top].astype(F32) + r_b1l[k].astype(F32)).astype(BF16)
        b2[k].append(start(s_a.at[i, top], r_b2l.at[k, top], right))
        b1[k][1].wait_recv()
        j = xk[3] * 4 + zk[k]
        s_a[j, low] = (s_a[j, low].astype(F32) + r_b1r[k].astype(F32)).astype(BF16)
        b2[k].append(start(s_a.at[j, low], r_b2r.at[k, low], left))

    def summed(k):
        for c in b2[k]:
            c.wait_recv()
        i = x * 4 + zk[k]
        return s_a[i].astype(F32) + (r_b2l[k].astype(F32) + r_b2r[k].astype(F32))

    def along_z(k):
        s_b[k] = summed(k).astype(BF16)
        c_z[k] = start(s_b.at[k], r_c.at[k], along[k])

    first(order[0])
    first(order[1])
    add_cores(1)
    add_cores(3)
    plain(order[0])
    for n in range(4):
        added(order[n])
        if n < 2:
            first(order[n + 2])
        if n < 3:
            plain(order[n + 1])
        if n == 0:
            add_cores(0)
        else:
            along_z(order[n - 1])
    total = summed(0)
    for k in (1, 2, 3):
        c_z[k].wait_recv()
        total = total + r_c[k].astype(F32)
    aggregate = total.astype(BF16)
    preact = jnp.dot(aggregate, w_ref[...], preferred_element_type=F32) + bias_ref[...]
    sig = jax.nn.sigmoid(preact)
    derivative = sig * (1.0 + preact * (1.0 - sig))
    grad_pre = (cot_ref[...].astype(F32) * derivative).astype(BF16)
    grad_agg = lax.dot_general(
        w_ref[...], grad_pre, (((1,), (1,)), ((), ())), preferred_element_type=F32
    ).astype(BF16)
    mine = (x * 4 + zl) * 2 + core
    full_ref[mine, 0] = grad_agg[:, 0:128]
    full_ref[mine, 1] = grad_agg[:, 128:256]

    def at(xx, zz):
        return (xx * 4 + zz) * 2 + core

    def ring(d):
        here = full_ref
        return (
            start(here.at[d, 0], here.at[d, 0], right),
            start(here.at[d, 1], here.at[d, 1], left),
            start(here.at[d, 1], here.at[d, 1], right),
            start(here.at[d, 0], here.at[d, 0], left),
        )

    def same(d, dev):
        return start(full_ref.at[d], full_ref.at[d], dev)

    def same_half(d, h, dev):
        return start(full_ref.at[d, h], full_ref.at[d, h], dev)

    z_in = {k: same(mine, along[k]) for k in (1, 2, 3)}
    rings = {0: ring(mine)}
    twins = [same(mine, twin)]
    zb = [rem4(zl + 4 - k) for k in range(4)]

    out_ref[...] = (preact * sig).astype(BF16)
    term_ref[:, 0:256] = lax.dot_general(
        aggregate, grad_pre, (((0,), (0,)), ((), ())), preferred_element_type=F32
    )
    term_ref[:, 256:384] = lax.dot_general(
        grad_pre, jnp.ones((256, 128), BF16), (((0,), (0,)), ((), ())), preferred_element_type=F32
    )

    yk = [rem4(y + k) for k in range(4)]

    def parameters():
        def at_row(row, n):
            return pl.ds(pl.multiple_of(row, n), n)

        half = at_row(core * 128, 128)
        c = start(term_ref.at[at_row((1 - core) * 128, 128)], t_c, twin)
        yield
        c.wait_recv()
        u_c[...] = term_ref[half] + t_c[...]
        cs = [start(u_c.at[at_row(yk[k] * 32, 32)], t_y.at[k], y_dev[k]) for k in (2, 1, 3)]
        yield
        for c in cs:
            c.wait_recv()
        u_y[...] = u_c[at_row(y * 32, 32)] + (t_y[1] + t_y[2] + t_y[3])
        cs = [start(u_y.at[at_row(xk[k] * 8, 8)], t_x.at[k], x_dev[k]) for k in (2, 1, 3)]
        yield
        for c in cs:
            c.wait_recv()
        u_x[...] = u_y[at_row(x * 8, 8)] + (t_x[1] + t_x[2] + t_x[3])
        cs = [start(u_x, t_z.at[zz], z_dev[k]) for k in (4, 3, 5, 2, 6, 1, 7)]
        t_z[zz] = u_x[...]
        yield
        for c in cs:
            c.wait_recv()
        value = t_z[0]
        for k in range(1, 8):
            value = value + t_z[k]
        spot = at_row(core * 128 + y * 32 + x * 8, 8)
        all_t[spot] = value * norm
        cs = [start(all_t.at[spot], all_t.at[spot], x_dev[k]) for k in (2, 1, 3)]
        yield
        for c in cs:
            c.wait_recv()
        spot = at_row(core * 128 + y * 32, 32)
        cs = [start(all_t.at[spot], all_t.at[spot], y_dev[k]) for k in (2, 1, 3)]
        yield
        for c in cs:
            c.wait_recv()
        c = start(all_t.at[half], all_t.at[half], twin)
        yield
        c.wait_recv()
        yield

    params = parameters()
    next(params)
    forwards = {}

    def relay(k):
        dl, dr = at(xk[3], zb[k]), at(xk[1], zb[k])
        rings[k][0].wait_recv()
        fr = same_half(dl, 0, right)
        rings[k][1].wait_recv()
        fl = same_half(dr, 1, left)
        forwards[k] = (fr, fl)

    def hand_over(k):
        dl, dr = at(xk[3], zb[k]), at(xk[1], zb[k])
        rings[k][2].wait_recv()
        twins.append(same(dl, twin))
        rings[k][3].wait_recv()
        twins.append(same(dr, twin))

    for k in range(4):
        relay(k)
        if k == 1:
            next(params)
        hand_over(k)
        if k > 0:
            next(params)
        if k < 3:
            d = at(x, zb[k + 1])
            z_in[k + 1].wait_recv()
            rings[k + 1] = ring(d)
            twins.append(same(d, twin))
        if k == 0:
            next(params)
    for k in range(4):
        if k == 3:
            next(params)
        d = at(xk[2], zb[k])
        forwards[k][0].wait_recv()
        twins.append(same_half(d, 0, twin))
        forwards[k][1].wait_recv()
        twins.append(same_half(d, 1, twin))
    for _ in params:
        pass
    for c in twins:
        c.wait_recv()
    for c in started:
        c.wait_send()


def middle(part, cot, weight, bias, norm):
    chunk = (256, 256)
    return pl.pallas_call(
        functools.partial(middle_kernel, norm),
        out_shape=(
            jax.ShapeDtypeStruct(chunk, BF16),
            jax.ShapeDtypeStruct((32, 2, 256, 128), BF16),
            jax.ShapeDtypeStruct((256, 384), F32),
        ),
        in_specs=[VMEM] * 4,
        out_specs=(VMEM,) * 3,
        scratch_shapes=[
            pltpu.VMEM((16,) + chunk, BF16),
            pltpu.VMEM((16,) + chunk, BF16),
            pltpu.VMEM((4, 128, 256), BF16),
            pltpu.VMEM((4, 128, 256), BF16),
            pltpu.VMEM((4,) + chunk, BF16),
            pltpu.VMEM((4,) + chunk, BF16),
            pltpu.VMEM((4,) + chunk, BF16),
            pltpu.VMEM((4,) + chunk, BF16),
            pltpu.VMEM((256, 384), F32),
            pltpu.VMEM((128, 384), F32),
            pltpu.VMEM((128, 384), F32),
            pltpu.VMEM((4, 32, 384), F32),
            pltpu.VMEM((32, 384), F32),
            pltpu.VMEM((4, 8, 384), F32),
            pltpu.VMEM((8, 384), F32),
            pltpu.VMEM((8, 8, 384), F32),
            pltpu.SemaphoreType.DMA((112,)),
            pltpu.SemaphoreType.DMA((112,)),
        ],
        compiler_params=pltpu.CompilerParams(
            collective_id=1, has_side_effects=True, vmem_limit_bytes=MIDDLE_VMEM
        ),
        name="layer",
    )(part, cot, weight, bias)


def backward_kernel(coords, live, a_ref, g_ref, o_ref, t_ref, out_ref, o_out, gw_out, gb_out, acc):
    n_cb = acc.shape[0] - 1
    o_out[...] = o_ref[...]
    gw_out[...] = t_ref[:, 0:256]
    gb_out[...] = t_ref[:, 256:384].T[0:1]

    def clear(i, _):
        acc[i] = jnp.zeros(acc.shape[1:], F32)
        return 0

    lax.fori_loop(0, n_cb, clear, 0)

    def some(q, _):
        products = []
        for u in range(UNROLL):
            s = q * UNROLL + u
            products.append(jnp.dot(g_ref[coords[0, s]], a_ref[s], preferred_element_type=F32))
        for u in range(UNROLL):
            s = q * UNROLL + u
            c = jnp.where(s < live[0, 0], coords[1, s], n_cb)
            acc[c] += products[u]
        return 0

    lax.fori_loop(0, (live[0, 0] + UNROLL - 1) // UNROLL, some, 0)
    for c in range(n_cb):
        out_ref[:, c * 128 : (c + 1) * 128] = acc[c].astype(BF16)


def backward_products(coords, live, blocks, grads, out, term):
    return pl.pallas_call(
        backward_kernel,
        out_shape=(
            jax.ShapeDtypeStruct((256, 2048), BF16),
            jax.ShapeDtypeStruct((256, 256), BF16),
            jax.ShapeDtypeStruct((256, 256), F32),
            jax.ShapeDtypeStruct((1, 256), F32),
        ),
        in_specs=[SMEM, SMEM, VMEM, VMEM, VMEM, VMEM],
        out_specs=(VMEM,) * 4,
        scratch_shapes=[pltpu.VMEM((17, 256, 128), F32)],
        compiler_params=pltpu.CompilerParams(vmem_limit_bytes=BACKWARD_VMEM),
        name="backward_products",
    )(coords, live, blocks, grads, out, term)


def finish_kernel(
    part, gx_ref, r_b1l, r_b1r, s_b1r, s_b1l, r_b2l, r_b2r, s_b, r_c, sends, recvs,
):
    zh, y, x, zl, core = place()
    right = device(zh, rem4(y + 1), x, zl, core)
    left = device(zh, rem4(y + 3), x, zl, core)
    across = device(1 - zh, y, x, zl, core)
    meet((left, right, across))
    started = []
    used = [0]

    def start(src, dst, dev):
        c = copy_to(src, dst, sends, recvs, used[0], dev)
        used[0] += 1
        c.start()
        started.append(c)
        return c

    yk = [rem4(y + k) for k in range(4)]
    top, low = pl.ds(0, 16), pl.ds(16, 16)

    zs = (1 - zh, zh)
    every = pl.ds(0, 16)
    pieces = ((0, pl.ds(0, 1024)), (0, pl.ds(1024, 1024)), (1, pl.ds(0, 2048)))
    b1, b2 = {}, {}

    def first(p):
        j, at = pieces[p]
        i = zs[j] * 4 + yk[2]
        b1[p] = (
            start(part.at[i, top, at], r_b1l.at[j, every, at], right),
            start(part.at[i, low, at], r_b1r.at[j, every, at], left),
        )

    def plain(p):
        j, at = pieces[p]
        b2[p] = [
            start(part.at[zs[j] * 4 + yk[1], low, at], r_b2l.at[j, low, at], right),
            start(part.at[zs[j] * 4 + yk[3], top, at], r_b2r.at[j, top, at], left),
        ]

    def added(p):
        j, at = pieces[p]
        b1[p][0].wait_recv()
        s_b1r[j, :, at] = (
            part[zs[j] * 4 + yk[1], top, at].astype(F32) + r_b1l[j, :, at].astype(F32)
        ).astype(BF16)
        b2[p].append(start(s_b1r.at[j, every, at], r_b2l.at[j, top, at], right))
        b1[p][1].wait_recv()
        s_b1l[j, :, at] = (
            part[zs[j] * 4 + yk[3], low, at].astype(F32) + r_b1r[j, :, at].astype(F32)
        ).astype(BF16)
        b2[p].append(start(s_b1l.at[j, every, at], r_b2r.at[j, low, at], left))

    def summed(p):
        j, at = pieces[p]
        for c in b2[p]:
            c.wait_recv()
        return part[zs[j] * 4 + y, :, at].astype(F32) + (
            r_b2l[j, :, at].astype(F32) + r_b2r[j, :, at].astype(F32)
        )

    def over(p):
        at = pieces[p][1]
        s_b[:, at] = summed(p).astype(BF16)
        return start(s_b.at[pl.ds(0, 32), at], r_c.at[pl.ds(0, 32), at], across)

    first(0)
    plain(0)
    first(1)
    added(0)
    plain(1)
    added(1)
    first(2)
    plain(2)
    cz = [over(0), over(1)]
    added(2)
    own = summed(2)
    for c in cz:
        c.wait_recv()
    gx_ref[...] = (own + r_c[...].astype(F32)).astype(BF16)
    for c in started:
        c.wait_send()


def finish(part):
    half, whole = (2, 16, 2048), (2, 32, 2048)
    return pl.pallas_call(
        finish_kernel,
        out_shape=jax.ShapeDtypeStruct((32, 2048), BF16),
        in_specs=[VMEM],
        out_specs=VMEM,
        scratch_shapes=[
            pltpu.VMEM(half, BF16),
            pltpu.VMEM(half, BF16),
            pltpu.VMEM(half, BF16),
            pltpu.VMEM(half, BF16),
            pltpu.VMEM(whole, BF16),
            pltpu.VMEM(whole, BF16),
            pltpu.VMEM(whole[1:], BF16),
            pltpu.VMEM(whole[1:], BF16),
            pltpu.SemaphoreType.DMA((24,)),
            pltpu.SemaphoreType.DMA((24,)),
        ],
        compiler_params=pltpu.CompilerParams(
            collective_id=2, has_side_effects=True, vmem_limit_bytes=FINISH_VMEM
        ),
        name="finish",
    )(part)


def on_device(features, block_values, block_coords, live_blocks, weight, bias, cotangent):
    blocks, coords = block_values[0, 0], block_coords[0, 0]
    nodes = features.shape[0] * lax.axis_size("col")
    x_t, blocks, coords = gather_rows(features.T, blocks, coords)
    part = forward_products(coords, live_blocks, blocks, x_t.reshape(256, 2048))
    out, grads, term = middle(part, cotangent, weight, bias[None], nodes**-0.5)
    part_x, out, grad_weight, grad_bias = backward_products(
        coords, live_blocks, blocks, grads.reshape(64, 256, 128), out, term
    )
    gx_t = finish(part_x.reshape(8, 32, 2048))
    return out, gx_t.T, grad_weight, grad_bias[0]


def solution(mesh):
    in_specs = (
        P("col", "row"),
        P("row", "col", None, None, None),
        P("row", "col", None, None),
        P("row", "col"),
        P(),
        P(),
        P(("row", "col"), None),
    )
    out_specs = (P(("row", "col"), None), P("col", "row"), P(), P())
    return jax.shard_map(
        on_device, mesh=mesh, in_specs=in_specs, out_specs=out_specs, check_vma=False
    )
```

```python
import functools

import jax
import jax.numpy as jnp
from jax import lax
from jax.experimental import pallas as pl
from jax.experimental.pallas import tpu as pltpu
from jax.sharding import PartitionSpec as P

MESH = pl.DeviceIdType.MESH
F32 = jnp.float32
BF16 = jnp.bfloat16
UNROLL = 32
VMEM = pl.BlockSpec(memory_space=pltpu.VMEM)
SMEM = pl.BlockSpec(memory_space=pltpu.SMEM)
ANY = pl.BlockSpec(memory_space=pltpu.HBM)
MIB = 2**20
GATHER_VMEM = 42 * MIB
FORWARD_VMEM = 24 * MIB
MIDDLE_VMEM = 24 * MIB
BACKWARD_VMEM = 20 * MIB
FINISH_VMEM = 6 * MIB


def place():
    row, col = lax.axis_index("row"), lax.axis_index("col")
    return row // 4, row % 4, col // 8, (col // 2) % 4, col % 2


def device(zh, y, x, zl, core):
    return (zh * 4 + y, (x * 4 + zl) * 2 + core)


def copy_to(src, dst, sends, recvs, at, dev):
    return pltpu.make_async_remote_copy(
        src_ref=src,
        dst_ref=dst,
        send_sem=sends.at[at],
        recv_sem=recvs.at[at],
        device_id=dev,
        device_id_type=MESH,
    )


def meet(devices):
    barrier = pltpu.get_barrier_semaphore()
    for dev in devices:
        pl.semaphore_signal(barrier, inc=1, device_id=dev, device_id_type=MESH)
    pl.semaphore_wait(barrier, len(devices))


def rem4(v):
    return lax.rem(v, 4)


def gather_rows_kernel(x_ref, b_ref, c_ref, full_ref, b_out, c_out, sends, recvs, locals_):
    zh, y, x, zl, core = place()
    right = device(zh, rem4(y + 1), x, zl, core)
    left = device(zh, rem4(y + 3), x, zl, core)
    across = device(1 - zh, y, x, zl, core)
    meet((left, right, across))
    mine = zh * 4 + y
    other = (1 - zh) * 4 + y
    staged = [
        pltpu.make_async_copy(src, dst, locals_.at[i])
        for i, (src, dst) in enumerate(((x_ref, full_ref.at[mine]), (b_ref, b_out), (c_ref, c_out)))
    ]
    halves = (pl.ds(0, 16), pl.ds(16, 16))
    started = []

    def start(c):
        c.start()
        started.append(c)
        return c

    zc = [
        start(copy_to(x_ref.at[h], full_ref.at[mine, h], sends, recvs, 12 + i, across))
        for i, h in enumerate(halves)
    ]
    forwards = []
    for k in range(2):
        me = mine if k == 0 else other
        base = (zh if k == 0 else 1 - zh) * 4
        src = x_ref if k == 0 else full_ref.at[other]

        def ring(h, at, dev):
            return start(
                copy_to(src.at[halves[h]], full_ref.at[me, halves[h]], sends, recvs, k * 6 + at, dev)
            )

        if k == 1:
            zc[0].wait_recv()
        r0 = ring(0, 0, right)
        if k == 1:
            zc[1].wait_recv()
        l1 = ring(1, 1, left)
        r1 = ring(1, 2, right)
        l0 = ring(0, 3, left)
        if k == 0:
            for c in staged:
                c.start()
        from_left = base + rem4(y + 3)
        from_right = base + rem4(y + 1)
        r0.wait_recv()
        fr = start(
            copy_to(
                full_ref.at[from_left, halves[0]],
                full_ref.at[from_left, halves[0]],
                sends,
                recvs,
                k * 6 + 4,
                right,
            )
        )
        l1.wait_recv()
        fl = start(
            copy_to(
                full_ref.at[from_right, halves[1]],
                full_ref.at[from_right, halves[1]],
                sends,
                recvs,
                k * 6 + 5,
                left,
            )
        )
        forwards += [r1, l0, fr, fl]
    for c in forwards:
        c.wait_recv()
    for c in staged:
        c.wait()
    for c in started:
        c.wait_send()


def gather_rows(x_t, blocks, coords):
    width, verts = x_t.shape
    return pl.pallas_call(
        gather_rows_kernel,
        out_shape=(
            jax.ShapeDtypeStruct((8, width, verts), BF16),
            jax.ShapeDtypeStruct(blocks.shape, BF16),
            jax.ShapeDtypeStruct(coords.shape, jnp.int32),
        ),
        in_specs=[ANY] * 3,
        out_specs=(VMEM,) * 3,
        scratch_shapes=[
            pltpu.SemaphoreType.DMA((14,)),
            pltpu.SemaphoreType.DMA((14,)),
            pltpu.SemaphoreType.DMA((3,)),
        ],
        compiler_params=pltpu.CompilerParams(
            collective_id=0, has_side_effects=True, vmem_limit_bytes=GATHER_VMEM
        ),
        name="gather_features",
    )(x_t, blocks, coords)


def forward_kernel(coords, live, a_ref, xt_ref, out_ref, xs, acc):
    n_rb = acc.shape[0] - 1
    n_cb = xs.shape[0]
    for c in range(n_cb):
        xs[c] = xt_ref[:, c * 128 : (c + 1) * 128].T

    def clear(i, _):
        acc[i] = jnp.zeros(acc.shape[1:], F32)
        return 0

    lax.fori_loop(0, n_rb, clear, 0)

    def some(q, _):
        products = []
        for u in range(UNROLL):
            s = q * UNROLL + u
            products.append(jnp.dot(a_ref[s], xs[coords[1, s]], preferred_element_type=F32))
        for u in range(UNROLL):
            s = q * UNROLL + u
            r = jnp.where(s < live[0, 0], coords[0, s], n_rb)
            acc[r] += products[u]
        return 0

    lax.fori_loop(0, (live[0, 0] + UNROLL - 1) // UNROLL, some, 0)

    def put(chip, _):
        for k in range(4):
            out_ref[k // 2, chip, (k % 2) * 128 : (k % 2 + 1) * 128, :] = acc[chip * 4 + k].astype(BF16)
        return 0

    lax.fori_loop(0, 16, put, 0)


def forward_products(coords, live, blocks, x_t):
    return pl.pallas_call(
        forward_kernel,
        out_shape=jax.ShapeDtypeStruct((2, 16, 256, 256), BF16),
        in_specs=[SMEM, SMEM, VMEM, VMEM],
        out_specs=VMEM,
        scratch_shapes=[pltpu.VMEM((16, 128, 256), BF16), pltpu.VMEM((65, 128, 256), F32)],
        compiler_params=pltpu.CompilerParams(vmem_limit_bytes=FORWARD_VMEM),
        name="forward_products",
    )(coords, live, blocks, x_t)


def middle_kernel(
    norm, part, cot_ref, w_ref, bias_ref, out_ref, full_ref, all_t,
    r_a, s_a, r_b1l, r_b1r, r_b2l, r_b2r, s_b, r_c,
    term_ref, t_c, u_c, t_y, u_y, t_x, u_x, t_z, sends, recvs,
):
    zh, y, x, zl, core = place()
    right = device(zh, y, rem4(x + 1), zl, core)
    left = device(zh, y, rem4(x + 3), zl, core)
    twin = device(zh, y, x, zl, 1 - core)
    along = [None] + [device(zh, y, x, rem4(zl + k), core) for k in range(1, 4)]
    y_dev = [None] + [device(zh, rem4(y + k), x, zl, core) for k in range(1, 4)]
    x_dev = [None] + [device(zh, y, rem4(x + k), zl, core) for k in range(1, 4)]
    zz = zh * 4 + zl
    z_dev = [None]
    for k in range(1, 8):
        other = lax.rem(zz + k, 8)
        z_dev.append(device(other // 4, y, x, lax.rem(other, 4), core))
    meet([twin] + y_dev[1:] + x_dev[1:] + z_dev[1:])
    started = []
    used = [0]

    def start(src, dst, dev):
        c = copy_to(src, dst, sends, recvs, used[0], dev)
        used[0] += 1
        c.start()
        started.append(c)
        return c

    top, low = pl.ds(0, 128), pl.ds(128, 128)
    xk = [rem4(x + k) for k in range(4)]
    zk = [rem4(zl + k) for k in range(4)]
    order = (2, 1, 3, 0)
    a = {}
    far = {}
    for k in order:
        i = xk[2] * 4 + zk[k]
        far[k] = start(part.at[1 - core, i], r_a.at[i], twin)
    for k in (1, 3, 0):
        sl = pl.ds(xk[k] * 4, 4)
        a[k] = start(part.at[1 - core, sl], r_a.at[sl], twin)

    def add_cores(k):
        a[k].wait_recv()

        def one(z, _):
            i = xk[k] * 4 + z
            s_a[i] = (part[core, i].astype(F32) + r_a[i].astype(F32)).astype(BF16)
            return 0

        lax.fori_loop(0, 4, one, 0)

    b1, b2, c_z = {}, {}, {}

    def first(k):
        i = xk[2] * 4 + zk[k]
        far[k].wait_recv()
        s_a[i] = (part[core, i].astype(F32) + r_a[i].astype(F32)).astype(BF16)
        b1[k] = (
            start(s_a.at[i, top], r_b1l.at[k], right),
            start(s_a.at[i, low], r_b1r.at[k], left),
        )

    def plain(k):
        b2[k] = [
            start(s_a.at[xk[1] * 4 + zk[k], low], r_b2l.at[k, low], right),
            start(s_a.at[xk[3] * 4 + zk[k], top], r_b2r.at[k, top], left),
        ]

    def added(k):
        b1[k][0].wait_recv()
        i = xk[1] * 4 + zk[k]
        s_a[i, top] = (s_a[i, top].astype(F32) + r_b1l[k].astype(F32)).astype(BF16)
        b2[k].append(start(s_a.at[i, top], r_b2l.at[k, top], right))
        b1[k][1].wait_recv()
        j = xk[3] * 4 + zk[k]
        s_a[j, low] = (s_a[j, low].astype(F32) + r_b1r[k].astype(F32)).astype(BF16)
        b2[k].append(start(s_a.at[j, low], r_b2r.at[k, low], left))

    def summed(k):
        for c in b2[k]:
            c.wait_recv()
        i = x * 4 + zk[k]
        return s_a[i].astype(F32) + (r_b2l[k].astype(F32) + r_b2r[k].astype(F32))

    def along_z(k):
        s_b[k] = summed(k).astype(BF16)
        c_z[k] = start(s_b.at[k], r_c.at[k], along[k])

    first(order[0])
    first(order[1])
    add_cores(1)
    add_cores(3)
    plain(order[0])
    for n in range(4):
        added(order[n])
        if n < 2:
            first(order[n + 2])
        if n < 3:
            plain(order[n + 1])
        if n == 0:
            add_cores(0)
        else:
            along_z(order[n - 1])
    total = summed(0)
    for k in (1, 2, 3):
        c_z[k].wait_recv()
        total = total + r_c[k].astype(F32)
    aggregate = total.astype(BF16)
    preact = jnp.dot(aggregate, w_ref[...], preferred_element_type=F32) + bias_ref[...]
    sig = jax.nn.sigmoid(preact)
    derivative = sig * (1.0 + preact * (1.0 - sig))
    grad_pre = (cot_ref[...].astype(F32) * derivative).astype(BF16)
    grad_agg = lax.dot_general(
        w_ref[...], grad_pre, (((1,), (1,)), ((), ())), preferred_element_type=F32
    ).astype(BF16)
    mine = (x * 4 + zl) * 2 + core
    full_ref[mine, 0] = grad_agg[:, 0:128]
    full_ref[mine, 1] = grad_agg[:, 128:256]

    def at(xx, zz):
        return (xx * 4 + zz) * 2 + core

    def ring(d):
        here = full_ref
        return (
            start(here.at[d, 0], here.at[d, 0], right),
            start(here.at[d, 1], here.at[d, 1], left),
            start(here.at[d, 1], here.at[d, 1], right),
            start(here.at[d, 0], here.at[d, 0], left),
        )

    def same(d, dev):
        return start(full_ref.at[d], full_ref.at[d], dev)

    def same_half(d, h, dev):
        return start(full_ref.at[d, h], full_ref.at[d, h], dev)

    z_in = {k: same(mine, along[k]) for k in (1, 2, 3)}
    rings = {0: ring(mine)}
    twins = [same(mine, twin)]
    zb = [rem4(zl + 4 - k) for k in range(4)]

    out_ref[...] = (preact * sig).astype(BF16)
    term_ref[:, 0:256] = lax.dot_general(
        aggregate, grad_pre, (((0,), (0,)), ((), ())), preferred_element_type=F32
    )
    term_ref[:, 256:384] = lax.dot_general(
        grad_pre, jnp.ones((256, 128), BF16), (((0,), (0,)), ((), ())), preferred_element_type=F32
    )

    yk = [rem4(y + k) for k in range(4)]

    def parameters():
        def at_row(row, n):
            return pl.ds(pl.multiple_of(row, n), n)

        half = at_row(core * 128, 128)
        c = start(term_ref.at[at_row((1 - core) * 128, 128)], t_c, twin)
        yield
        c.wait_recv()
        u_c[...] = term_ref[half] + t_c[...]
        cs = [start(u_c.at[at_row(yk[k] * 32, 32)], t_y.at[k], y_dev[k]) for k in (2, 1, 3)]
        yield
        for c in cs:
            c.wait_recv()
        u_y[...] = u_c[at_row(y * 32, 32)] + (t_y[1] + t_y[2] + t_y[3])
        cs = [start(u_y.at[at_row(xk[k] * 8, 8)], t_x.at[k], x_dev[k]) for k in (2, 1, 3)]
        yield
        for c in cs:
            c.wait_recv()
        u_x[...] = u_y[at_row(x * 8, 8)] + (t_x[1] + t_x[2] + t_x[3])
        cs = [start(u_x, t_z.at[zz], z_dev[k]) for k in (4, 3, 5, 2, 6, 1, 7)]
        t_z[zz] = u_x[...]
        yield
        for c in cs:
            c.wait_recv()
        value = t_z[0]
        for k in range(1, 8):
            value = value + t_z[k]
        spot = at_row(core * 128 + y * 32 + x * 8, 8)
        all_t[spot] = value * norm
        cs = [start(all_t.at[spot], all_t.at[spot], x_dev[k]) for k in (2, 1, 3)]
        yield
        for c in cs:
            c.wait_recv()
        spot = at_row(core * 128 + y * 32, 32)
        cs = [start(all_t.at[spot], all_t.at[spot], y_dev[k]) for k in (2, 1, 3)]
        yield
        for c in cs:
            c.wait_recv()
        c = start(all_t.at[half], all_t.at[half], twin)
        yield
        c.wait_recv()
        yield

    params = parameters()
    next(params)
    forwards = {}

    def relay(k):
        dl, dr = at(xk[3], zb[k]), at(xk[1], zb[k])
        rings[k][0].wait_recv()
        fr = same_half(dl, 0, right)
        rings[k][1].wait_recv()
        fl = same_half(dr, 1, left)
        forwards[k] = (fr, fl)

    def hand_over(k):
        dl, dr = at(xk[3], zb[k]), at(xk[1], zb[k])
        rings[k][2].wait_recv()
        twins.append(same(dl, twin))
        rings[k][3].wait_recv()
        twins.append(same(dr, twin))

    for k in range(4):
        relay(k)
        if k == 1:
            next(params)
        hand_over(k)
        if k > 0:
            next(params)
        if k < 3:
            d = at(x, zb[k + 1])
            z_in[k + 1].wait_recv()
            rings[k + 1] = ring(d)
            twins.append(same(d, twin))
        if k == 0:
            next(params)
    for k in range(4):
        if k == 3:
            next(params)
        d = at(xk[2], zb[k])
        forwards[k][0].wait_recv()
        twins.append(same_half(d, 0, twin))
        forwards[k][1].wait_recv()
        twins.append(same_half(d, 1, twin))
    for _ in params:
        pass
    for c in twins:
        c.wait_recv()
    for c in started:
        c.wait_send()


def middle(part, cot, weight, bias, norm):
    chunk = (256, 256)
    return pl.pallas_call(
        functools.partial(middle_kernel, norm),
        out_shape=(
            jax.ShapeDtypeStruct(chunk, BF16),
            jax.ShapeDtypeStruct((32, 2, 256, 128), BF16),
            jax.ShapeDtypeStruct((256, 384), F32),
        ),
        in_specs=[VMEM] * 4,
        out_specs=(VMEM,) * 3,
        scratch_shapes=[
            pltpu.VMEM((16,) + chunk, BF16),
            pltpu.VMEM((16,) + chunk, BF16),
            pltpu.VMEM((4, 128, 256), BF16),
            pltpu.VMEM((4, 128, 256), BF16),
            pltpu.VMEM((4,) + chunk, BF16),
            pltpu.VMEM((4,) + chunk, BF16),
            pltpu.VMEM((4,) + chunk, BF16),
            pltpu.VMEM((4,) + chunk, BF16),
            pltpu.VMEM((256, 384), F32),
            pltpu.VMEM((128, 384), F32),
            pltpu.VMEM((128, 384), F32),
            pltpu.VMEM((4, 32, 384), F32),
            pltpu.VMEM((32, 384), F32),
            pltpu.VMEM((4, 8, 384), F32),
            pltpu.VMEM((8, 384), F32),
            pltpu.VMEM((8, 8, 384), F32),
            pltpu.SemaphoreType.DMA((112,)),
            pltpu.SemaphoreType.DMA((112,)),
        ],
        compiler_params=pltpu.CompilerParams(
            collective_id=1, has_side_effects=True, vmem_limit_bytes=MIDDLE_VMEM
        ),
        name="layer",
    )(part, cot, weight, bias)


def backward_kernel(coords, live, a_ref, g_ref, o_ref, t_ref, out_ref, o_out, gw_out, gb_out, acc):
    n_cb = acc.shape[0] - 1
    o_out[...] = o_ref[...]
    gw_out[...] = t_ref[:, 0:256]
    gb_out[...] = t_ref[:, 256:384].T[0:1]

    def clear(i, _):
        acc[i] = jnp.zeros(acc.shape[1:], F32)
        return 0

    lax.fori_loop(0, n_cb, clear, 0)

    def some(q, _):
        products = []
        for u in range(UNROLL):
            s = q * UNROLL + u
            products.append(jnp.dot(g_ref[coords[0, s]], a_ref[s], preferred_element_type=F32))
        for u in range(UNROLL):
            s = q * UNROLL + u
            c = jnp.where(s < live[0, 0], coords[1, s], n_cb)
            acc[c] += products[u]
        return 0

    lax.fori_loop(0, (live[0, 0] + UNROLL - 1) // UNROLL, some, 0)
    for c in range(n_cb):
        out_ref[:, c * 128 : (c + 1) * 128] = acc[c].astype(BF16)


def backward_products(coords, live, blocks, grads, out, term):
    return pl.pallas_call(
        backward_kernel,
        out_shape=(
            jax.ShapeDtypeStruct((256, 2048), BF16),
            jax.ShapeDtypeStruct((256, 256), BF16),
            jax.ShapeDtypeStruct((256, 256), F32),
            jax.ShapeDtypeStruct((1, 256), F32),
        ),
        in_specs=[SMEM, SMEM, VMEM, VMEM, VMEM, VMEM],
        out_specs=(VMEM,) * 4,
        scratch_shapes=[pltpu.VMEM((17, 256, 128), F32)],
        compiler_params=pltpu.CompilerParams(vmem_limit_bytes=BACKWARD_VMEM),
        name="backward_products",
    )(coords, live, blocks, grads, out, term)


def finish_kernel(
    part, gx_ref, r_b1l, r_b1r, s_b1r, s_b1l, r_b2l, r_b2r, s_b, r_c, sends, recvs,
):
    zh, y, x, zl, core = place()
    right = device(zh, rem4(y + 1), x, zl, core)
    left = device(zh, rem4(y + 3), x, zl, core)
    across = device(1 - zh, y, x, zl, core)
    meet((left, right, across))
    started = []
    used = [0]

    def start(src, dst, dev):
        c = copy_to(src, dst, sends, recvs, used[0], dev)
        used[0] += 1
        c.start()
        started.append(c)
        return c

    yk = [rem4(y + k) for k in range(4)]
    top, low = pl.ds(0, 16), pl.ds(16, 16)

    zs = (1 - zh, zh)
    every = pl.ds(0, 16)
    pieces = ((0, pl.ds(0, 1024)), (0, pl.ds(1024, 1024)), (1, pl.ds(0, 2048)))
    b1, b2 = {}, {}

    def first(p):
        j, at = pieces[p]
        i = zs[j] * 4 + yk[2]
        b1[p] = (
            start(part.at[i, top, at], r_b1l.at[j, every, at], right),
            start(part.at[i, low, at], r_b1r.at[j, every, at], left),
        )

    def plain(p):
        j, at = pieces[p]
        b2[p] = [
            start(part.at[zs[j] * 4 + yk[1], low, at], r_b2l.at[j, low, at], right),
            start(part.at[zs[j] * 4 + yk[3], top, at], r_b2r.at[j, top, at], left),
        ]

    def added(p):
        j, at = pieces[p]
        b1[p][0].wait_recv()
        s_b1r[j, :, at] = (
            part[zs[j] * 4 + yk[1], top, at].astype(F32) + r_b1l[j, :, at].astype(F32)
        ).astype(BF16)
        b2[p].append(start(s_b1r.at[j, every, at], r_b2l.at[j, top, at], right))
        b1[p][1].wait_recv()
        s_b1l[j, :, at] = (
            part[zs[j] * 4 + yk[3], low, at].astype(F32) + r_b1r[j, :, at].astype(F32)
        ).astype(BF16)
        b2[p].append(start(s_b1l.at[j, every, at], r_b2r.at[j, low, at], left))

    def summed(p):
        j, at = pieces[p]
        for c in b2[p]:
            c.wait_recv()
        return part[zs[j] * 4 + y, :, at].astype(F32) + (
            r_b2l[j, :, at].astype(F32) + r_b2r[j, :, at].astype(F32)
        )

    def over(p):
        at = pieces[p][1]
        s_b[:, at] = summed(p).astype(BF16)
        return start(s_b.at[pl.ds(0, 32), at], r_c.at[pl.ds(0, 32), at], across)

    first(0)
    plain(0)
    first(1)
    added(0)
    plain(1)
    added(1)
    first(2)
    plain(2)
    cz = [over(0), over(1)]
    added(2)
    own = summed(2)
    for c in cz:
        c.wait_recv()
    gx_ref[...] = (own + r_c[...].astype(F32)).astype(BF16)
    for c in started:
        c.wait_send()


def finish(part):
    half, whole = (2, 16, 2048), (2, 32, 2048)
    return pl.pallas_call(
        finish_kernel,
        out_shape=jax.ShapeDtypeStruct((32, 2048), BF16),
        in_specs=[VMEM],
        out_specs=VMEM,
        scratch_shapes=[
            pltpu.VMEM(half, BF16),
            pltpu.VMEM(half, BF16),
            pltpu.VMEM(half, BF16),
            pltpu.VMEM(half, BF16),
            pltpu.VMEM(whole, BF16),
            pltpu.VMEM(whole, BF16),
            pltpu.VMEM(whole[1:], BF16),
            pltpu.VMEM(whole[1:], BF16),
            pltpu.SemaphoreType.DMA((24,)),
            pltpu.SemaphoreType.DMA((24,)),
        ],
        compiler_params=pltpu.CompilerParams(
            collective_id=2, has_side_effects=True, vmem_limit_bytes=FINISH_VMEM
        ),
        name="finish",
    )(part)


def on_device(features, block_values, block_coords, live_blocks, weight, bias, cotangent):
    blocks, coords = block_values[0, 0], block_coords[0, 0]
    nodes = features.shape[0] * lax.axis_size("col")
    x_t, blocks, coords = gather_rows(features.T, blocks, coords)
    part = forward_products(coords, live_blocks, blocks, x_t.reshape(256, 2048))
    out, grads, term = middle(part, cotangent, weight, bias[None], nodes**-0.5)
    part_x, out, grad_weight, grad_bias = backward_products(
        coords, live_blocks, blocks, grads.reshape(64, 256, 128), out, term
    )
    gx_t = finish(part_x.reshape(8, 32, 2048))
    return out, gx_t.T, grad_weight, grad_bias[0]


def solution(mesh):
    in_specs = (
        P("col", "row"),
        P("row", "col", None, None, None),
        P("row", "col", None, None),
        P("row", "col"),
        P(),
        P(),
        P(("row", "col"), None),
    )
    out_specs = (P(("row", "col"), None), P("col", "row"), P(), P())
    return jax.shard_map(
        on_device, mesh=mesh, in_specs=in_specs, out_specs=out_specs, check_vma=False
    )
```
